32 devices in a mesh: dp: 8 (over z, y), mp: 4 (over x, core).
Axes of the slice: x: 2, y: 2, z: 4, core: 2. Of those that a mesh axis runs over, the one named last changes fastest.
Arguments:
- grads: bfloat16 [8, 16384, 1024], P('dp', None, 'mp'), may hold values from -1000 to 1000
- weights: float32 [16384, 1024], P('dp', 'mp'), may hold values from -6 to 6
- moment1: float32 [16384, 1024], P('dp', 'mp'), may hold values from -6 to 6
- moment2: float32 [16384, 1024], P('dp', 'mp'), may hold values from 0.01 to 4
- average: bfloat16 [16384, 1024], P('dp', 'mp'), may hold values from -6 to 6
- owners: int32 [64, 1], replicated, may hold values from 0 to 7, as said below
Outputs:
- new_weights: float32 [16384, 1024], P(None, 'mp')
- new_moment1: float32 [16384, 1024], P('dp', 'mp')
- new_moment2: float32 [16384, 1024], P('dp', 'mp')
- owned_average: bfloat16 [8, 3072, 1024], P('dp', None, 'mp')
The draws below stay inside these ranges and needn't reach their ends.
Inputs may be any that keep to these rules, and one draw needn't show every extreme that they name: `owners`: every dp index keeps at least one matrix and at most 12, and some keeps exactly 12. Of the matrices whose rows lie on one dp index, at most 2 are kept by any one dp index, and in every draw some dp index keeps exactly 2 of one dp index's matrices.
All inputs are finite; a program needn't handle non-finite values.
Results may differ from the reference program's by a relative error of at most 0.007.
Values may be sent and summed in bfloat16 or wider, within the bound.
A program may use at most 192 MiB of HBM per device.

```python
import math
import jax
import jax.numpy as jnp
from jax import lax

D = 1024
BLOCK = 256
EMAT = 32
NMAT = 64
ROWS = 16384
MOST = 12
N_DP = 8


def draw_grads(key, part):
    keys = jax.random.split(key, 3)
    row_pos = jnp.arange(ROWS, dtype=jnp.float32) / ROWS
    col_pos = jnp.arange(D, dtype=jnp.float32) / D
    row_scale = jnp.exp(jax.random.uniform(keys[1], (1, ROWS, 1), jnp.float32) * math.log(10.0))
    col_scale = jnp.exp(jax.random.uniform(keys[2], (1, 1, D), jnp.float32) * math.log(10.0))
    rising = (3.0 ** row_pos)[None, :, None] * (3.0 ** col_pos)[None, None, :]
    base = jax.random.normal(keys[0], (N_DP, ROWS, D), jnp.float32)
    values = base * row_scale * col_scale * rising / 40.0
    return jnp.clip(values, -1000.0, 1000.0).astype(jnp.bfloat16)


def draw_owners(key, part):
    dev_count = N_DP
    per_dev = NMAT // N_DP
    pair_count = per_dev // 2
    key_perm, key_target, key_flip = jax.random.split(jax.random.fold_in(key, 7), 3)
    order_perm = jax.random.permutation(key_perm, dev_count).astype(jnp.int32)
    target = jax.random.randint(key_target, (), 0, dev_count, dtype=jnp.int32)
    flip_bits = jax.random.randint(key_flip, (dev_count, pair_count), 0, 2, dtype=jnp.int32)
    local_ids = jnp.arange(per_dev, dtype=jnp.int32)
    shifts = order_perm[local_ids % dev_count]
    sender = jnp.arange(dev_count, dtype=jnp.int32)[:, None]
    base_owner = (sender + shifts[None, :]) % dev_count
    even_shift = shifts[0:2 * pair_count:2]
    odd_shift = shifts[1:2 * pair_count:2]
    send_in = (target - even_shift) % dev_count
    send_out = (target - odd_shift) % dev_count
    flip_bits = jnp.where(sender == send_in[None, :], 1, flip_bits)
    flip_bits = jnp.where(sender == send_out[None, :], 0, flip_bits)
    even_cols = base_owner[:, 0:2 * pair_count:2]
    odd_cols = jnp.where(flip_bits == 1, even_cols, base_owner[:, 1:2 * pair_count:2])
    paired = jnp.stack([even_cols, odd_cols], axis=2).reshape(dev_count, 2 * pair_count)
    owner_ids = jnp.concatenate([paired, base_owner[:, 2 * pair_count:]], axis=1)
    return owner_ids.reshape(NMAT, 1).astype(jnp.int32)


def steps_of(own_key, extent, shards, low, high):
    loudness = 1.0
    for axis_at, blocks in shards:
        steps = jax.random.uniform(jax.random.fold_in(jax.random.fold_in(own_key, 6), axis_at), (blocks,), jnp.float32, low / len(shards), high / len(shards))
        loudness = loudness * jnp.repeat(jnp.exp(steps), extent[axis_at] // blocks).reshape((-1,) + (1,) * (len(extent) - 1 - axis_at))
    return loudness


def gaussian(own_key, extent, width, reach, cuts=(), held_as=jnp.bfloat16):
    drawn = width * jax.random.normal(own_key, extent, jnp.float32)
    if cuts:
        drawn = drawn * steps_of(own_key, extent, cuts, -0.22, 0.18)
    return jnp.clip(drawn, -reach, reach).astype(held_as)


def setup_inputs(seed: int = 0) -> dict:
    key_list = jax.random.split(jax.random.key(seed), 7)
    return {
        "grads": draw_grads(jax.random.fold_in(key_list[6], 71), 0),
        "weights": gaussian(key_list[1], (ROWS, D), 1.0, 6.0, ((0, 8), (1, 4)), jnp.float32),
        "moment1": gaussian(key_list[2], (ROWS, D), 1.0, 6.0, ((0, 8), (1, 4)), jnp.float32),
        "moment2": jnp.clip(jnp.exp(math.log(4.0) - 5.9914646 * jax.random.uniform(key_list[3], (ROWS, D), jnp.float32) ** steps_of(key_list[3], (ROWS, D), ((0, 8), (1, 4)), -0.2, 0.2)), 0.01, 4.0),
        "average": gaussian(key_list[4], (ROWS, D), 1.0, 6.0, ((0, 8), (1, 4))),
        "owners": draw_owners(jax.random.fold_in(key_list[6], 71), 0),
    }


learning = 0.05
beta_one = 0.9
beta_two = 0.95
epsilon = 1e-08
weight_decay = 0.1
average_decay = 0.9
step_count = 10

def update(clipped, weights, moment1, moment2, row_ids):
    new_m = beta_one * moment1 + (1.0 - beta_one) * clipped
    new_v = beta_two * moment2 + (1.0 - beta_two) * clipped * clipped
    m_hat = new_m / (1.0 - beta_one ** step_count)
    v_hat = new_v / (1.0 - beta_two ** step_count)
    matrix_id = row_ids // BLOCK
    decayed = ((matrix_id != 4) & (matrix_id < NMAT - EMAT)).astype(jnp.float32)[:, None]
    new_w = weights - learning * (m_hat / (jnp.sqrt(v_hat) + epsilon) + weight_decay * decayed * weights)
    return (new_w, new_m, new_v)

def pick_owned(fresh_full, owner_col, owner_id, most):
    flags = owner_col == owner_id
    position = jnp.cumsum(flags.astype(jnp.int32)) - 1
    slots = jnp.arange(most, dtype=jnp.int32)
    select = (flags[None, :] & (position[None, :] == slots[:, None])).astype(jnp.bfloat16)
    stacked = fresh_full.reshape(NMAT, -1)
    picked = jnp.dot(select, stacked, preferred_element_type=jnp.float32)
    return picked.astype(jnp.bfloat16).reshape(most * BLOCK, -1)

def reference(grads, weights, moment1, moment2, average, owners):
    summed = lax.optimization_barrier(jnp.sum(grads, axis=0, dtype=jnp.float32))
    total = jnp.sum(summed * summed)
    limit = float(ROWS * D) ** 0.5
    factor = jnp.minimum(1.0, limit / (jnp.sqrt(total) + 1e-06))
    row_ids = jnp.arange(ROWS, dtype=jnp.int32)
    new_w, new_m, new_v = update(summed * factor, weights, moment1, moment2, row_ids)
    fresh = (average_decay * average.astype(jnp.float32) + (1.0 - average_decay) * new_w).astype(jnp.bfloat16)
    owner_col = owners[:, 0]
    owned = lax.map(lambda owner_id: pick_owned(fresh, owner_col, owner_id, MOST), jnp.arange(N_DP, dtype=jnp.int32))
    return (new_w, new_m, new_v, owned)
```

```python
import functools

import jax
import jax.numpy as jnp
from jax import lax
from jax.experimental import pallas as pl
from jax.experimental.pallas import tpu as pltpu
from jax.sharding import PartitionSpec as P

BLOCK = 256
EMAT = 32
MESH = pl.DeviceIdType.MESH


learning = 0.05
beta_one = 0.9
beta_two = 0.95
epsilon = 1e-08
weight_decay = 0.1
average_decay = 0.9
step_count = 10


def update(clipped, weights, moment1, moment2, decayed):
    new_m = beta_one * moment1 + (1.0 - beta_one) * clipped
    new_v = beta_two * moment2 + (1.0 - beta_two) * clipped * clipped
    m_hat = new_m / (1.0 - beta_one**step_count)
    v_hat = new_v / (1.0 - beta_two**step_count)
    new_w = weights - learning * (
        m_hat / (jnp.sqrt(v_hat) + epsilon) + weight_decay * decayed * weights
    )
    return (new_w, new_m, new_v)


def pick_owned(fresh_full, owner_col, owner_id, most, nmat):
    flags = owner_col == owner_id
    ids = jnp.arange(nmat, dtype=jnp.int32)
    position = jnp.sum((flags[None, :] & (ids[None, :] <= ids[:, None])).astype(jnp.int32), axis=1) - 1
    slots = jnp.arange(most, dtype=jnp.int32)
    select = (flags[None, :] & (position[None, :] == slots[:, None])).astype(jnp.bfloat16)
    stacked = fresh_full.reshape(nmat, -1)
    picked = jnp.dot(select, stacked, preferred_element_type=jnp.float32)
    return picked.astype(jnp.bfloat16).reshape(1, most * BLOCK, -1)


def plain_shards(limit, grads, weights, moment1, moment2, average, owners):
    shard_rows = weights.shape[0]
    local_count = shard_rows // BLOCK
    most = local_count + local_count // 2
    nmat = owners.shape[0]
    my_index = lax.axis_index("dp")
    summed = lax.psum_scatter(grads[0], "dp", scatter_dimension=0, tiled=True).astype(jnp.float32)
    total = lax.psum(jnp.sum(summed * summed), ("dp", "mp"))
    factor = jnp.minimum(1.0, limit / (jnp.sqrt(total) + 1e-06))
    row_ids = my_index * shard_rows + jnp.arange(shard_rows, dtype=jnp.int32)
    matrix_id = row_ids // BLOCK
    decayed = ((matrix_id != 4) & (matrix_id < nmat - EMAT)).astype(jnp.float32)[:, None]
    new_w, new_m, new_v = update(summed * factor, weights, moment1, moment2, decayed)
    new_full = lax.all_gather(new_w, "dp", axis=0, tiled=True)
    fresh = (average_decay * average.astype(jnp.float32) + (1.0 - average_decay) * new_w).astype(
        jnp.bfloat16
    )
    fresh_full = lax.all_gather(fresh, "dp", axis=0, tiled=True)
    owned = pick_owned(fresh_full, owners[:, 0], my_index, most, nmat)
    return (new_full, new_m, new_v, owned)


CHUNKS = 8
HALF = CHUNKS // 2
LEAD = 2
PER = 2
DIRECT_AT = 2
RELAY_AT = 12
PAIR_AT = 10
WINDOW = 10
TILE = 64


def step_kernel(
    n_dp, n_mp, limit, nmat,
    owners, grads, weights, moment1, moment2, average,
    gathered, out_m, out_v, unpacked,
    own, from_y, from_z, summed, w_buf, m_buf, v_buf, new_buf, part_dp, part_mp, other, from_p,
    kept, packed, relay,
    load_sem, y_send, y_recv, z_send, z_recv, dp_send, dp_recv, mp_send, mp_recv,
    a_send, a_recv, a_local, r_send, r_recv, f_send, gy_send, go_send, gf_send, g_recv, g_local, o_sem, p_send, p_recv, gp_send,
):
    me = lax.axis_index("dp")
    col = lax.axis_index("mp")
    z, y = me // 2, me % 2
    partner = me + 1 - 2 * y
    shard = weights.shape[0]
    rows = shard // CHUNKS
    width = weights.shape[1]
    mid = (z == 1) | (z == 2)
    end = (z == 0) | (z == 3)

    barrier = pltpu.get_barrier_semaphore()
    for k in range(1, n_dp):
        pl.semaphore_signal(
            barrier, inc=1, device_id=(lax.rem(me + k, n_dp), col), device_id_type=MESH
        )
    for k in range(1, n_mp):
        pl.semaphore_signal(
            barrier, inc=1, device_id=(me, lax.rem(col + k, n_mp)), device_id_type=MESH
        )

    order = [3 * (1 - z // 2), (2 + 3 * z) % 5, 1 + z % 2, z]
    hop_a = 2 * (1 - 2 * (z // 2))
    hop_b = 2 * (1 - 2 * (z % 2))
    hops = [hop_a, hop_b, hop_a]
    pair = z + 1 - 2 * (z % 2)

    loads = []
    for i in range(4):
        t = order[i]
        loads.append(
            pltpu.make_async_copy(
                grads.at[0, pl.ds((t * 2 + y) * shard, shard)], own.at[t], load_sem.at[i]
            )
        )
        loads[-1].start()
    state = []
    for i, (src, dst) in enumerate(((weights, w_buf), (moment1, m_buf), (moment2, v_buf))):
        state.append(pltpu.make_async_copy(src, dst, load_sem.at[4 + i]))

    other_load = pltpu.make_async_copy(
        grads.at[0, pl.ds((z * 2 + 1 - y) * shard, shard)], other, load_sem.at[7]
    )
    other_load.start()
    kept_load = pltpu.make_async_copy(average, kept, load_sem.at[8])
    kept_load.start()

    pl.semaphore_wait(barrier, n_dp - 1 + n_mp - 1)

    def not_paired(i, c, fn):
        if i == 1:
            pl.when(end)(fn)
        elif c < HALF and i == 2:
            pl.when(mid)(fn)
        else:
            fn()

    def p_copy(c):
        return pltpu.make_async_remote_copy(
            src_ref=grads.at[0, pl.ds((pair * 2 + 1 - y) * shard + c * rows, rows)],
            dst_ref=from_p.at[pl.ds(c * rows, rows)],
            send_sem=p_send.at[c],
            recv_sem=p_recv.at[c],
            device_id=(me + hop_b, col),
            device_id_type=MESH,
        )

    def y_copy(n):
        t, c = order[n // CHUNKS], n % CHUNKS
        if n // CHUNKS == 3:
            src = other.at[pl.ds(c * rows, rows)]
        else:
            src = grads.at[0, pl.ds((t * 2 + 1 - y) * shard + c * rows, rows)]
        return pltpu.make_async_remote_copy(
            src_ref=src,
            dst_ref=from_y.at[t, pl.ds(c * rows, rows)],
            send_sem=y_send.at[n],
            recv_sem=y_recv.at[n],
            device_id=(partner, col),
            device_id_type=MESH,
        )

    def z_copy(i, c):
        t = order[i]
        slot = t if i < 2 else t + (4 - t) * (z // 2)
        return pltpu.make_async_remote_copy(
            src_ref=own.at[t, pl.ds(c * rows, rows)],
            dst_ref=from_z.at[slot, pl.ds(c * rows, rows)],
            send_sem=z_send.at[i * CHUNKS + c],
            recv_sem=z_recv.at[slot * CHUNKS + c],
            device_id=(me + hops[i], col),
            device_id_type=MESH,
        )

    def z_wait(slot, c):
        pltpu.make_async_remote_copy(
            src_ref=own.at[0, pl.ds(c * rows, rows)],
            dst_ref=from_z.at[slot, pl.ds(c * rows, rows)],
            send_sem=z_send.at[0],
            recv_sem=z_recv.at[slot * CHUNKS + c],
            device_id=(partner, col),
            device_id_type=MESH,
        ).wait_recv()

    def f32(ref, at, start):
        return ref[at, pl.ds(start, TILE), :].astype(jnp.float32)

    slots = 2
    far = (3 - z) * 2
    local = kept.shape[0]

    def pack():
        for dst in range(n_dp):
            first, second, count = jnp.int32(0), jnp.int32(0), jnp.int32(0)
            for k in range(local):
                hit = (owners[me * local + k] == dst).astype(jnp.int32)
                first += hit * (count == 0).astype(jnp.int32) * k
                second += hit * (count == 1).astype(jnp.int32) * k
                count += hit
            packed[dst * slots] = kept[first]
            packed[dst * slots + 1] = kept[second]

    def a_send_copy(src_ref, src, dst, sem):
        return pltpu.make_async_remote_copy(
            src_ref=src_ref,
            dst_ref=unpacked.at[pl.ds(src * slots, slots)],
            send_sem=sem,
            recv_sem=a_recv.at[src],
            device_id=(dst, col),
            device_id_type=MESH,
        )

    def a_copy(dst):
        return a_send_copy(packed.at[pl.ds(dst * slots, slots)], me, dst, a_send.at[dst])

    def a_wait(k):
        src = lax.rem(me + k, n_dp)
        a_send_copy(packed.at[pl.ds(0, slots)], src, partner, a_send.at[0]).wait_recv()

    def r_copy(k):
        dst = 6 * k + 1 - y
        return pltpu.make_async_remote_copy(
            src_ref=packed.at[pl.ds(dst * slots, slots)],
            dst_ref=relay.at[pl.ds(k * slots, slots)],
            send_sem=r_send.at[k],
            recv_sem=r_recv.at[k],
            device_id=(partner, col),
            device_id_type=MESH,
        )

    def f_copy(k):
        return a_send_copy(relay.at[pl.ds(k * slots, slots)], partner, 6 * k + y, f_send.at[k])

    early = [y, 6 + y, far + y]
    middle = [partner, far + 1 - y]
    late = [2, 3, 4, 5]

    total_chunks = 4 * CHUNKS
    def y_start(n):
        if n < total_chunks:
            not_paired(n // CHUNKS, n % CHUNKS, lambda: y_copy(n).start())

    for n in range(WINDOW):
        y_start(n)
    for c in range(HALF):
        p_copy(c).start()
    kept_load.wait()
    pack()

    @pl.when(mid)
    def _():
        for c in range(HALF, CHUNKS):
            p_copy(c).start()
        for k in range(2):
            r_copy(k).start()

    for s in state:
        s.start()

    for n in range(3 * CHUNKS):
        i, c = n // CHUNKS, n % CHUNKS
        t = order[i]
        if c == 0:
            loads[i].wait()
        if n == DIRECT_AT:

            @pl.when(mid)
            def _():
                for dst in early:
                    a_copy(dst).start()

        if n == RELAY_AT:

            @pl.when(mid)
            def _():
                for k in range(2):
                    r_copy(k).wait_recv()
                    f_copy(k).start()

        if n == PAIR_AT:
            other_load.wait()
        k = n - PAIR_AT
        if 0 <= k < CHUNKS:

            def join():
                p_copy(k).wait_recv()

                @pl.loop(0, rows // TILE)
                def _(b):
                    part = pl.ds(pl.multiple_of(k * rows + b * TILE, TILE), TILE)
                    val = other[part, :].astype(jnp.float32) + from_p[part, :].astype(jnp.float32)
                    other[part, :] = val.astype(jnp.bfloat16)

            if k < HALF:
                join()
            else:
                pl.when(end)(join)

        not_paired(i, c, lambda: y_copy(n).wait_recv())
        y_start(n + WINDOW)

        def add(with_y, with_z):
            if with_z:
                z_wait(t, c)

            @pl.loop(0, rows // TILE)
            def _(b):
                at = pl.multiple_of(c * rows + b * TILE, TILE)
                val = f32(own, t, at)
                if with_y:
                    val = val + f32(from_y, t, at)
                if with_z:
                    val = val + f32(from_z, t, at)
                own[t, pl.ds(at, TILE), :] = val.astype(jnp.bfloat16)

        paired_mid = i == 1
        paired_end = c < HALF and i == 2
        pl.when(mid)(functools.partial(add, not paired_mid, True))
        if not paired_end:
            pl.when(end)(functools.partial(add, True, False))
        z_copy(i, c).start()

    loads[3].wait()
    part_dp[me] = jnp.zeros((8, width), jnp.float32)
    for c in range(CHUNKS):
        n = 3 * CHUNKS + c
        y_copy(n).wait_recv()
        y_start(n + WINDOW)
        z_wait(z, c)

        def keep(at, val):
            summed[pl.ds(at, TILE), :] = val
            part_dp[me] += jnp.sum((val * val).reshape(TILE // 8, 8, width), axis=0)

        @pl.when(mid)
        def _():
            z_wait(4, c)

            @pl.loop(0, rows // TILE)
            def _(b):
                at = pl.multiple_of(c * rows + b * TILE, TILE)
                keep(at, f32(own, z, at) + f32(from_y, z, at) + f32(from_z, z, at) + f32(from_z, 4, at))

        @pl.when(end)
        def _():
            @pl.loop(0, rows // TILE)
            def _(b):
                at = pl.multiple_of(c * rows + b * TILE, TILE)
                keep(at, f32(own, z, at) + f32(from_y, z, at) + f32(from_z, z, at))

    def dp_copy(k):
        return pltpu.make_async_remote_copy(
            src_ref=part_dp.at[me],
            dst_ref=part_dp.at[me],
            send_sem=dp_send.at[k],
            recv_sem=dp_recv.at[me],
            device_id=(lax.rem(me + k, n_dp), col),
            device_id_type=MESH,
        )

    def dp_wait(k):
        src = lax.rem(me + k, n_dp)
        pltpu.make_async_remote_copy(
            src_ref=part_dp.at[src],
            dst_ref=part_dp.at[src],
            send_sem=dp_send.at[k],
            recv_sem=dp_recv.at[src],
            device_id=(src, col),
            device_id_type=MESH,
        ).wait_recv()

    def mp_copy(k):
        return pltpu.make_async_remote_copy(
            src_ref=part_mp.at[col],
            dst_ref=part_mp.at[col],
            send_sem=mp_send.at[k],
            recv_sem=mp_recv.at[col],
            device_id=(me, lax.rem(col + k, n_mp)),
            device_id_type=MESH,
        )

    def mp_wait(k):
        src = lax.rem(col + k, n_mp)
        pltpu.make_async_remote_copy(
            src_ref=part_mp.at[src],
            dst_ref=part_mp.at[src],
            send_sem=mp_send.at[k],
            recv_sem=mp_recv.at[src],
            device_id=(me, src),
            device_id_type=MESH,
        ).wait_recv()

    for k in range(1, n_dp):
        dp_copy(k).start()
    a_own = pltpu.make_async_copy(
        packed.at[pl.ds(me * slots, slots)], unpacked.at[pl.ds(me * slots, slots)], a_local.at[0]
    )
    a_own.start()
    for dst in middle:
        a_copy(dst).start()

    @pl.when(end)
    def _():
        a_copy(far + y).start()

    for k in range(1, n_dp):
        dp_wait(k)
    group = part_dp[0]
    for k in range(1, n_dp):
        group = group + part_dp[k]
    part_mp[col] = group
    for k in range(1, n_mp):
        mp_copy(k).start()
    for s in state:
        s.wait()
    for k in range(1, n_mp):
        mp_wait(k)
    everything = part_mp[0]
    for k in range(1, n_mp):
        everything = everything + part_mp[k]
    total = jnp.sum(everything, axis=(0, 1), keepdims=True)
    factor = jnp.minimum(1.0, limit / (jnp.sqrt(total) + 1e-06))

    def g_copy(src_ref, dev, c, send_sem, target):
        return pltpu.make_async_remote_copy(
            src_ref=src_ref,
            dst_ref=gathered.at[pl.ds(dev * shard + c * rows, rows)],
            send_sem=send_sem,
            recv_sem=g_recv.at[dev * CHUNKS + c],
            device_id=(target, col),
            device_id_type=MESH,
        )

    def own_y(c):
        return g_copy(new_buf.at[pl.ds(c * rows, rows)], me, c, gy_send.at[c], partner)

    def own_z(c, hop, j):
        return g_copy(new_buf.at[pl.ds(c * rows, rows)], me, c, go_send.at[j * CHUNKS + c], me + hop)

    def fwd_y(i, c):
        dev = order[i] * 2 + y
        src = gathered.at[pl.ds(dev * shard + c * rows, rows)]
        return g_copy(src, dev, c, gy_send.at[(i + 1) * CHUNKS + c], partner)

    def fwd_z(i, c):
        dev = order[i] * 2 + y
        src = gathered.at[pl.ds(dev * shard + c * rows, rows)]
        return g_copy(src, dev, c, gf_send.at[i * CHUNKS + c], me - hops[i])

    def fwd_p(c):
        dev = z * 2 + 1 - y
        src = gathered.at[pl.ds(dev * shard + c * rows, rows)]
        return g_copy(src, dev, c, gp_send.at[c], me + hop_b)

    def g_wait(dev, c):
        g_copy(new_buf.at[pl.ds(c * rows, rows)], dev, c, gy_send.at[0], partner).wait_recv()

    def local_copies(c):
        part = pl.ds(c * rows, rows)
        return [
            pltpu.make_async_copy(
                new_buf.at[part], gathered.at[pl.ds(me * shard + c * rows, rows)], g_local.at[c]
            ),
            pltpu.make_async_copy(m_buf.at[part], out_m.at[part], o_sem.at[c]),
            pltpu.make_async_copy(v_buf.at[part], out_v.at[part], o_sem.at[CHUNKS + c]),
        ]

    for c in range(CHUNKS):

        @pl.loop(0, rows // TILE)
        def _(b):
            at = pl.multiple_of(c * rows + b * TILE, TILE)
            matrix_id = (me * shard + at) // BLOCK
            decayed = jnp.where((matrix_id != 4) & (matrix_id < nmat - EMAT), 1.0, 0.0)
            part = pl.ds(at, TILE)
            new_w, new_m, new_v = update(
                summed[part, :] * factor, w_buf[part, :], m_buf[part, :], v_buf[part, :], decayed
            )
            m_buf[part, :] = new_m
            v_buf[part, :] = new_v
            new_buf[part, :] = new_w.astype(jnp.bfloat16)

        own_y(c).start()

        @pl.when(z < 3)
        def _():
            own_z(c, 2, 0).start()

        @pl.when(z > 0)
        def _():
            own_z(c, -2, 1).start()

        for copy in local_copies(c):
            copy.start()

    @pl.when(end)
    def _():
        for dst in late:
            a_copy(dst).start()

    for i in (2, 1, 0):
        for c in range(CHUNKS):
            g_wait(order[i] * 2 + y, c)

            @pl.when(mid)
            def _():
                fwd_z(i, c).start()

            not_paired(i, c, lambda: fwd_y(i, c).start())
            if i == 2:

                def pass_on():
                    g_wait(z * 2 + 1 - y, c)
                    fwd_p(c).start()

                if c < HALF:
                    pass_on()
                else:
                    pl.when(end)(pass_on)

    for i in range(4):
        for c in range(CHUNKS):
            if i < 3:
                g_wait(order[i] * 2 + 1 - y, c)
            elif c >= HALF:
                pl.when(mid)(lambda: g_wait(z * 2 + 1 - y, c))
    for n in range(total_chunks):
        not_paired(n // CHUNKS, n % CHUNKS, lambda: y_copy(n).wait_send())
    for i in range(3):
        for c in range(CHUNKS):
            z_copy(i, c).wait_send()
            not_paired(i, c, lambda: fwd_y(i, c).wait_send())
    for c in range(CHUNKS):
        if c < HALF:
            p_copy(c).wait_send()
            fwd_p(c).wait_send()
        else:
            pl.when(mid)(lambda: p_copy(c).wait_send())
            pl.when(end)(lambda: fwd_p(c).wait_send())
    for k in range(1, n_dp):
        dp_copy(k).wait_send()
        a_wait(k)
    for dst in middle:
        a_copy(dst).wait_send()

    @pl.when(end)
    def _():
        a_copy(far + y).wait_send()
        for dst in late:
            a_copy(dst).wait_send()

    @pl.when(mid)
    def _():
        for dst in early:
            a_copy(dst).wait_send()
        for k in range(2):
            r_copy(k).wait_send()
            f_copy(k).wait_send()

    a_own.wait()
    for k in range(1, n_mp):
        mp_copy(k).wait_send()
    for c in range(CHUNKS):
        own_y(c).wait_send()
        for copy in local_copies(c):
            copy.wait()

    @pl.when(z < 3)
    def _():
        for c in range(CHUNKS):
            own_z(c, 2, 0).wait_send()

    @pl.when(z > 0)
    def _():
        for c in range(CHUNKS):
            own_z(c, -2, 1).wait_send()

    @pl.when(mid)
    def _():
        for i in range(3):
            for c in range(CHUNKS):
                fwd_z(i, c).wait_send()


def finish_kernel(
    n_dp, most, nmat, owners, block, m_in, v_in, gathered, unpacked,
    out_w, owned, m_out, v_out, a_buf, w_buf, count, sem, state_sem
):
    step = pl.program_id(0)
    me = lax.axis_index("dp")
    local = nmat // n_dp

    def copies(slot, a_from, g):
        return (
            pltpu.make_async_copy(unpacked.at[a_from], a_buf.at[slot], sem.at[slot]),
            pltpu.make_async_copy(
                gathered.at[pl.ds(g * BLOCK, BLOCK)], w_buf.at[slot], sem.at[most + slot]
            ),
        )

    state = [
        pltpu.make_async_copy(m_in, m_out, state_sem.at[0]),
        pltpu.make_async_copy(v_in, v_out, state_sem.at[1]),
    ]

    @pl.when(step == 0)
    def _():
        for copy in state:
            copy.start()

        def scan(src, kept):
            def one(k, carry):
                kept, here = carry
                g = src * local + k
                mine = owners[g] == me

                @pl.when(mine)
                def _():
                    for copy in copies(kept, src * 2 + here, g):
                        copy.start()

                inc = mine.astype(jnp.int32)
                return kept + inc, here + inc

            return lax.fori_loop(0, local, one, (kept, jnp.int32(0)))[0]

        count[0] = lax.fori_loop(0, n_dp, scan, jnp.int32(0))

    out_w[...] = block[...].astype(jnp.float32)

    for j in range(PER):
        slot = (step - LEAD) * PER + j
        part = pl.ds(j * BLOCK, BLOCK)

        @pl.when((slot >= 0) & (slot < count[0]))
        def _():
            for copy in copies(slot, 0, 0):
                copy.wait()
            fresh = average_decay * a_buf[slot].astype(jnp.float32) + (
                1.0 - average_decay
            ) * w_buf[slot].astype(jnp.float32)
            owned[0, part, :] = fresh.astype(jnp.bfloat16)

        @pl.when((slot >= count[0]) & (slot >= 0) & (slot < most))
        def _():
            owned[0, part, :] = jnp.zeros((BLOCK, owned.shape[2]), jnp.bfloat16)

    @pl.when(step == n_dp - 1)
    def _():
        for copy in state:
            copy.wait()


def grid_shards(n_dp, n_mp, limit, grads, weights, moment1, moment2, average, owners):
    shard, width = weights.shape
    local = shard // BLOCK
    most = local + local // 2
    nmat = owners.shape[0]
    total_rows = grads.shape[1]
    owner_col = owners[:, 0]
    any_spec = pl.BlockSpec(memory_space=pl.ANY)
    smem_spec = pl.BlockSpec(memory_space=pltpu.SMEM)
    bf16, f32 = jnp.bfloat16, jnp.float32
    dma = pltpu.SemaphoreType.DMA

    average = average.reshape(local, BLOCK, width)
    grads, weights, moment1, moment2, average = (
        pltpu.with_memory_space_constraint(a, pltpu.HBM)
        for a in (grads, weights, moment1, moment2, average)
    )
    gathered, new_m, new_v, unpacked = pl.pallas_call(
        functools.partial(step_kernel, n_dp, n_mp, limit, nmat),
        out_shape=(
            pltpu.VMEM((total_rows, width), bf16),
            pltpu.VMEM((shard, width), f32),
            pltpu.VMEM((shard, width), f32),
            pltpu.VMEM((n_dp * 2, BLOCK, width), bf16),
        ),
        in_specs=[smem_spec] + [any_spec] * 5,
        out_specs=(any_spec,) * 4,
        scratch_shapes=[
            pltpu.VMEM((4, shard, width), bf16),
            pltpu.VMEM((4, shard, width), bf16),
            pltpu.VMEM((5, shard, width), bf16),
            pltpu.VMEM((shard, width), f32),
            pltpu.VMEM((shard, width), f32),
            pltpu.VMEM((shard, width), f32),
            pltpu.VMEM((shard, width), f32),
            pltpu.VMEM((shard, width), bf16),
            pltpu.VMEM((n_dp, 8, width), f32),
            pltpu.VMEM((n_mp, 8, width), f32),
            pltpu.VMEM((shard, width), bf16),
            pltpu.VMEM((shard, width), bf16),
            pltpu.VMEM((local, BLOCK, width), bf16),
            pltpu.VMEM((n_dp * 2, BLOCK, width), bf16),
            pltpu.VMEM((4, BLOCK, width), bf16),
            dma((9,)),
            dma((4 * CHUNKS,)),
            dma((4 * CHUNKS,)),
            dma((3 * CHUNKS,)),
            dma((5 * CHUNKS,)),
            dma((n_dp,)),
            dma((n_dp,)),
            dma((n_mp,)),
            dma((n_mp,)),
            dma((n_dp,)),
            dma((n_dp,)),
            dma((1,)),
            dma((2,)),
            dma((2,)),
            dma((2,)),
            dma((4 * CHUNKS,)),
            dma((2 * CHUNKS,)),
            dma((3 * CHUNKS,)),
            dma((n_dp * CHUNKS,)),
            dma((CHUNKS,)),
            dma((2 * CHUNKS,)),
            dma((CHUNKS,)),
            dma((CHUNKS,)),
            dma((CHUNKS,)),
        ],
        compiler_params=pltpu.CompilerParams(
            collective_id=0, has_side_effects=True, vmem_limit_bytes=32 * 2**20
        ),
    )(owner_col, grads, weights, moment1, moment2, average)

    gathered, new_m, new_v, unpacked = (
        pltpu.with_memory_space_constraint(a, pltpu.VMEM) for a in (gathered, new_m, new_v, unpacked)
    )
    new_full, owned, new_m, new_v = pl.pallas_call(
        functools.partial(finish_kernel, n_dp, most, nmat),
        grid=(n_dp,),
        out_shape=(
            jax.ShapeDtypeStruct((total_rows, width), f32),
            jax.ShapeDtypeStruct((1, most * BLOCK, width), bf16),
            jax.ShapeDtypeStruct((shard, width), f32),
            jax.ShapeDtypeStruct((shard, width), f32),
        ),
        in_specs=[
            smem_spec,
            pl.BlockSpec((shard, width), lambda i: (i, 0)),
            any_spec,
            any_spec,
            any_spec,
            any_spec,
        ],
        out_specs=(
            pl.BlockSpec((shard, width), lambda i: (i, 0)),
            pl.BlockSpec(
                (1, PER * BLOCK, width), lambda i: (0, jnp.clip(i - LEAD, 0, most // PER - 1), 0)
            ),
            any_spec,
            any_spec,
        ),
        scratch_shapes=[
            pltpu.VMEM((most, BLOCK, width), bf16),
            pltpu.VMEM((most, BLOCK, width), bf16),
            pltpu.SMEM((1,), jnp.int32),
            dma((2 * most,)),
            dma((2,)),
        ],
        compiler_params=pltpu.CompilerParams(vmem_limit_bytes=24 * 2**20),
    )(owner_col, gathered, new_m, new_v, gathered, unpacked)
    return (new_full, new_m, new_v, owned)


def solution(mesh):
    n_dp, n_mp = mesh.shape["dp"], mesh.shape["mp"]

    def step(grads, weights, moment1, moment2, average, owners):
        limit = float(weights.shape[0] * weights.shape[1]) ** 0.5
        if n_dp == 8:
            body = functools.partial(grid_shards, n_dp, n_mp, limit)
        else:
            body = functools.partial(plain_shards, limit)
        placed = (P("dp", None, "mp"), P("dp", "mp"), P("dp", "mp"), P("dp", "mp"), P("dp", "mp"), P())
        return jax.shard_map(
            body,
            mesh=mesh,
            in_specs=placed,
            out_specs=(P(None, "mp"), P("dp", "mp"), P("dp", "mp"), P("dp", None, "mp")),
            check_vma=False,
        )(grads, weights, moment1, moment2, average, owners)

    return step
```

```python
import functools

import jax
import jax.numpy as jnp
from jax import lax
from jax.experimental import pallas as pl
from jax.experimental.pallas import tpu as pltpu
from jax.sharding import PartitionSpec as P

BLOCK = 256
EMAT = 32
MESH = pl.DeviceIdType.MESH


learning = 0.05
beta_one = 0.9
beta_two = 0.95
epsilon = 1e-08
weight_decay = 0.1
average_decay = 0.9
step_count = 10


def update(clipped, weights, moment1, moment2, decayed):
    new_m = beta_one * moment1 + (1.0 - beta_one) * clipped
    new_v = beta_two * moment2 + (1.0 - beta_two) * clipped * clipped
    m_hat = new_m / (1.0 - beta_one**step_count)
    v_hat = new_v / (1.0 - beta_two**step_count)
    new_w = weights - learning * (
        m_hat / (jnp.sqrt(v_hat) + epsilon) + weight_decay * decayed * weights
    )
    return (new_w, new_m, new_v)


def pick_owned(fresh_full, owner_col, owner_id, most, nmat):
    flags = owner_col == owner_id
    ids = jnp.arange(nmat, dtype=jnp.int32)
    position = jnp.sum((flags[None, :] & (ids[None, :] <= ids[:, None])).astype(jnp.int32), axis=1) - 1
    slots = jnp.arange(most, dtype=jnp.int32)
    select = (flags[None, :] & (position[None, :] == slots[:, None])).astype(jnp.bfloat16)
    stacked = fresh_full.reshape(nmat, -1)
    picked = jnp.dot(select, stacked, preferred_element_type=jnp.float32)
    return picked.astype(jnp.bfloat16).reshape(1, most * BLOCK, -1)


def plain_shards(limit, grads, weights, moment1, moment2, average, owners):
    shard_rows = weights.shape[0]
    local_count = shard_rows // BLOCK
    most = local_count + local_count // 2
    nmat = owners.shape[0]
    my_index = lax.axis_index("dp")
    summed = lax.psum_scatter(grads[0], "dp", scatter_dimension=0, tiled=True).astype(jnp.float32)
    total = lax.psum(jnp.sum(summed * summed), ("dp", "mp"))
    factor = jnp.minimum(1.0, limit / (jnp.sqrt(total) + 1e-06))
    row_ids = my_index * shard_rows + jnp.arange(shard_rows, dtype=jnp.int32)
    matrix_id = row_ids // BLOCK
    decayed = ((matrix_id != 4) & (matrix_id < nmat - EMAT)).astype(jnp.float32)[:, None]
    new_w, new_m, new_v = update(summed * factor, weights, moment1, moment2, decayed)
    new_full = lax.all_gather(new_w, "dp", axis=0, tiled=True)
    fresh = (average_decay * average.astype(jnp.float32) + (1.0 - average_decay) * new_w).astype(
        jnp.bfloat16
    )
    fresh_full = lax.all_gather(fresh, "dp", axis=0, tiled=True)
    owned = pick_owned(fresh_full, owners[:, 0], my_index, most, nmat)
    return (new_full, new_m, new_v, owned)


CHUNKS = 8
HALF = CHUNKS // 2
PART = 1024
DEPTH = 4
DIRECT_AT = 2
RELAY_AT = 12
PAIR_AT = 10
WINDOW = 10
TILE = 64


def step_kernel(
    n_dp, n_mp, limit, nmat,
    owners, grads, weights, moment1, moment2, average,
    gathered, out_m, out_v, unpacked,
    own, from_y, from_z, summed, w_buf, m_buf, v_buf, new_buf, part_dp, part_mp, other, from_p,
    kept, packed, relay,
    load_sem, y_send, y_recv, z_send, z_recv, dp_send, dp_recv, mp_send, mp_recv,
    a_send, a_recv, a_local, r_send, r_recv, f_send, gy_send, go_send, gf_send, g_recv, g_local, o_sem, p_send, p_recv, gp_send,
):
    me = lax.axis_index("dp")
    col = lax.axis_index("mp")
    z, y = me // 2, me % 2
    partner = me + 1 - 2 * y
    shard = weights.shape[0]
    rows = shard // CHUNKS
    width = weights.shape[1]
    mid = (z == 1) | (z == 2)
    end = (z == 0) | (z == 3)

    barrier = pltpu.get_barrier_semaphore()
    for k in range(1, n_dp):
        pl.semaphore_signal(
            barrier, inc=1, device_id=(lax.rem(me + k, n_dp), col), device_id_type=MESH
        )
    for k in range(1, n_mp):
        pl.semaphore_signal(
            barrier, inc=1, device_id=(me, lax.rem(col + k, n_mp)), device_id_type=MESH
        )

    order = [3 * (1 - z // 2), (2 + 3 * z) % 5, 1 + z % 2, z]
    hop_a = 2 * (1 - 2 * (z // 2))
    hop_b = 2 * (1 - 2 * (z % 2))
    hops = [hop_a, hop_b, hop_a]
    pair = z + 1 - 2 * (z % 2)

    loads = []
    for i in range(4):
        t = order[i]
        loads.append(
            pltpu.make_async_copy(
                grads.at[0, pl.ds((t * 2 + y) * shard, shard)], own.at[t], load_sem.at[i]
            )
        )
        loads[-1].start()
    state = []
    for i, (src, dst) in enumerate(((weights, w_buf), (moment1, m_buf), (moment2, v_buf))):
        state.append(pltpu.make_async_copy(src, dst, load_sem.at[4 + i]))

    other_load = pltpu.make_async_copy(
        grads.at[0, pl.ds((z * 2 + 1 - y) * shard, shard)], other, load_sem.at[7]
    )
    other_load.start()
    kept_load = pltpu.make_async_copy(average, kept, load_sem.at[8])
    kept_load.start()

    pl.semaphore_wait(barrier, n_dp - 1 + n_mp - 1)

    def not_paired(i, c, fn):
        if i == 1:
            pl.when(end)(fn)
        elif c < HALF and i == 2:
            pl.when(mid)(fn)
        else:
            fn()

    def p_copy(c):
        return pltpu.make_async_remote_copy(
            src_ref=grads.at[0, pl.ds((pair * 2 + 1 - y) * shard + c * rows, rows)],
            dst_ref=from_p.at[pl.ds(c * rows, rows)],
            send_sem=p_send.at[c],
            recv_sem=p_recv.at[c],
            device_id=(me + hop_b, col),
            device_id_type=MESH,
        )

    def y_copy(n):
        t, c = order[n // CHUNKS], n % CHUNKS
        if n // CHUNKS == 3:
            src = other.at[pl.ds(c * rows, rows)]
        else:
            src = grads.at[0, pl.ds((t * 2 + 1 - y) * shard + c * rows, rows)]
        return pltpu.make_async_remote_copy(
            src_ref=src,
            dst_ref=from_y.at[t, pl.ds(c * rows, rows)],
            send_sem=y_send.at[n],
            recv_sem=y_recv.at[n],
            device_id=(partner, col),
            device_id_type=MESH,
        )

    def z_copy(i, c):
        t = order[i]
        slot = t if i < 2 else t + (4 - t) * (z // 2)
        return pltpu.make_async_remote_copy(
            src_ref=own.at[t, pl.ds(c * rows, rows)],
            dst_ref=from_z.at[slot, pl.ds(c * rows, rows)],
            send_sem=z_send.at[i * CHUNKS + c],
            recv_sem=z_recv.at[slot * CHUNKS + c],
            device_id=(me + hops[i], col),
            device_id_type=MESH,
        )

    def z_wait(slot, c):
        pltpu.make_async_remote_copy(
            src_ref=own.at[0, pl.ds(c * rows, rows)],
            dst_ref=from_z.at[slot, pl.ds(c * rows, rows)],
            send_sem=z_send.at[0],
            recv_sem=z_recv.at[slot * CHUNKS + c],
            device_id=(partner, col),
            device_id_type=MESH,
        ).wait_recv()

    def f32(ref, at, start):
        return ref[at, pl.ds(start, TILE), :].astype(jnp.float32)

    slots = 2
    far = (3 - z) * 2
    local = kept.shape[0]

    def pack():
        for dst in range(n_dp):
            first, second, count = jnp.int32(0), jnp.int32(0), jnp.int32(0)
            for k in range(local):
                hit = (owners[me * local + k] == dst).astype(jnp.int32)
                first += hit * (count == 0).astype(jnp.int32) * k
                second += hit * (count == 1).astype(jnp.int32) * k
                count += hit
            packed[dst * slots] = kept[first]
            packed[dst * slots + 1] = kept[second]

    def a_send_copy(src_ref, src, dst, sem):
        return pltpu.make_async_remote_copy(
            src_ref=src_ref,
            dst_ref=unpacked.at[pl.ds(src * slots, slots)],
            send_sem=sem,
            recv_sem=a_recv.at[src],
            device_id=(dst, col),
            device_id_type=MESH,
        )

    def a_copy(dst):
        return a_send_copy(packed.at[pl.ds(dst * slots, slots)], me, dst, a_send.at[dst])

    def a_wait(k):
        src = lax.rem(me + k, n_dp)
        a_send_copy(packed.at[pl.ds(0, slots)], src, partner, a_send.at[0]).wait_recv()

    def r_copy(k):
        dst = 6 * k + 1 - y
        return pltpu.make_async_remote_copy(
            src_ref=packed.at[pl.ds(dst * slots, slots)],
            dst_ref=relay.at[pl.ds(k * slots, slots)],
            send_sem=r_send.at[k],
            recv_sem=r_recv.at[k],
            device_id=(partner, col),
            device_id_type=MESH,
        )

    def f_copy(k):
        return a_send_copy(relay.at[pl.ds(k * slots, slots)], partner, 6 * k + y, f_send.at[k])

    early = [y, 6 + y, far + y]
    middle = [partner, far + 1 - y]
    late = [2, 3, 4, 5]

    total_chunks = 4 * CHUNKS
    def y_start(n):
        if n < total_chunks:
            not_paired(n // CHUNKS, n % CHUNKS, lambda: y_copy(n).start())

    for n in range(WINDOW):
        y_start(n)
    for c in range(HALF):
        p_copy(c).start()
    kept_load.wait()
    pack()

    @pl.when(mid)
    def _():
        for c in range(HALF, CHUNKS):
            p_copy(c).start()
        for k in range(2):
            r_copy(k).start()

    for s in state:
        s.start()

    for n in range(3 * CHUNKS):
        i, c = n // CHUNKS, n % CHUNKS
        t = order[i]
        if c == 0:
            loads[i].wait()
        if n == DIRECT_AT:

            @pl.when(mid)
            def _():
                for dst in early:
                    a_copy(dst).start()

        if n == RELAY_AT:

            @pl.when(mid)
            def _():
                for k in range(2):
                    r_copy(k).wait_recv()
                    f_copy(k).start()

        if n == PAIR_AT:
            other_load.wait()
        k = n - PAIR_AT
        if 0 <= k < CHUNKS:

            def join():
                p_copy(k).wait_recv()

                @pl.loop(0, rows // TILE)
                def _(b):
                    part = pl.ds(pl.multiple_of(k * rows + b * TILE, TILE), TILE)
                    val = other[part, :].astype(jnp.float32) + from_p[part, :].astype(jnp.float32)
                    other[part, :] = val.astype(jnp.bfloat16)

            if k < HALF:
                join()
            else:
                pl.when(end)(join)

        not_paired(i, c, lambda: y_copy(n).wait_recv())
        y_start(n + WINDOW)

        def add(with_y, with_z):
            if with_z:
                z_wait(t, c)

            @pl.loop(0, rows // TILE)
            def _(b):
                at = pl.multiple_of(c * rows + b * TILE, TILE)
                val = f32(own, t, at)
                if with_y:
                    val = val + f32(from_y, t, at)
                if with_z:
                    val = val + f32(from_z, t, at)
                own[t, pl.ds(at, TILE), :] = val.astype(jnp.bfloat16)

        paired_mid = i == 1
        paired_end = c < HALF and i == 2
        pl.when(mid)(functools.partial(add, not paired_mid, True))
        if not paired_end:
            pl.when(end)(functools.partial(add, True, False))
        z_copy(i, c).start()

    loads[3].wait()
    part_dp[me] = jnp.zeros((8, width), jnp.float32)
    for c in range(CHUNKS):
        n = 3 * CHUNKS + c
        y_copy(n).wait_recv()
        y_start(n + WINDOW)
        z_wait(z, c)

        def keep(at, val):
            summed[pl.ds(at, TILE), :] = val
            part_dp[me] += jnp.sum((val * val).reshape(TILE // 8, 8, width), axis=0)

        @pl.when(mid)
        def _():
            z_wait(4, c)

            @pl.loop(0, rows // TILE)
            def _(b):
                at = pl.multiple_of(c * rows + b * TILE, TILE)
                keep(at, f32(own, z, at) + f32(from_y, z, at) + f32(from_z, z, at) + f32(from_z, 4, at))

        @pl.when(end)
        def _():
            @pl.loop(0, rows // TILE)
            def _(b):
                at = pl.multiple_of(c * rows + b * TILE, TILE)
                keep(at, f32(own, z, at) + f32(from_y, z, at) + f32(from_z, z, at))

    def dp_copy(k):
        return pltpu.make_async_remote_copy(
            src_ref=part_dp.at[me],
            dst_ref=part_dp.at[me],
            send_sem=dp_send.at[k],
            recv_sem=dp_recv.at[me],
            device_id=(lax.rem(me + k, n_dp), col),
            device_id_type=MESH,
        )

    def dp_wait(k):
        src = lax.rem(me + k, n_dp)
        pltpu.make_async_remote_copy(
            src_ref=part_dp.at[src],
            dst_ref=part_dp.at[src],
            send_sem=dp_send.at[k],
            recv_sem=dp_recv.at[src],
            device_id=(src, col),
            device_id_type=MESH,
        ).wait_recv()

    def mp_copy(k):
        return pltpu.make_async_remote_copy(
            src_ref=part_mp.at[col],
            dst_ref=part_mp.at[col],
            send_sem=mp_send.at[k],
            recv_sem=mp_recv.at[col],
            device_id=(me, lax.rem(col + k, n_mp)),
            device_id_type=MESH,
        )

    def mp_wait(k):
        src = lax.rem(col + k, n_mp)
        pltpu.make_async_remote_copy(
            src_ref=part_mp.at[src],
            dst_ref=part_mp.at[src],
            send_sem=mp_send.at[k],
            recv_sem=mp_recv.at[src],
            device_id=(me, src),
            device_id_type=MESH,
        ).wait_recv()

    for k in range(1, n_dp):
        dp_copy(k).start()
    a_own = pltpu.make_async_copy(
        packed.at[pl.ds(me * slots, slots)], unpacked.at[pl.ds(me * slots, slots)], a_local.at[0]
    )
    a_own.start()
    for k in range(1, n_dp):
        dp_wait(k)
    group = part_dp[0]
    for k in range(1, n_dp):
        group = group + part_dp[k]
    part_mp[col] = group
    for k in range(1, n_mp):
        mp_copy(k).start()
    for dst in middle:
        a_copy(dst).start()

    @pl.when(end)
    def _():
        a_copy(far + y).start()

    for s in state:
        s.wait()
    for k in range(1, n_mp):
        mp_wait(k)
    everything = part_mp[0]
    for k in range(1, n_mp):
        everything = everything + part_mp[k]
    total = jnp.sum(everything, axis=(0, 1), keepdims=True)
    factor = jnp.minimum(1.0, limit / (jnp.sqrt(total) + 1e-06))

    def g_copy(src_ref, dev, c, send_sem, target):
        return pltpu.make_async_remote_copy(
            src_ref=src_ref,
            dst_ref=gathered.at[pl.ds(dev * shard + c * rows, rows)],
            send_sem=send_sem,
            recv_sem=g_recv.at[dev * CHUNKS + c],
            device_id=(target, col),
            device_id_type=MESH,
        )

    def own_y(c):
        return g_copy(new_buf.at[pl.ds(c * rows, rows)], me, c, gy_send.at[c], partner)

    def own_z(c, hop, j):
        return g_copy(new_buf.at[pl.ds(c * rows, rows)], me, c, go_send.at[j * CHUNKS + c], me + hop)

    def fwd_y(i, c):
        dev = order[i] * 2 + y
        src = gathered.at[pl.ds(dev * shard + c * rows, rows)]
        return g_copy(src, dev, c, gy_send.at[(i + 1) * CHUNKS + c], partner)

    def fwd_z(i, c):
        dev = order[i] * 2 + y
        src = gathered.at[pl.ds(dev * shard + c * rows, rows)]
        return g_copy(src, dev, c, gf_send.at[i * CHUNKS + c], me - hops[i])

    def fwd_p(c):
        dev = z * 2 + 1 - y
        src = gathered.at[pl.ds(dev * shard + c * rows, rows)]
        return g_copy(src, dev, c, gp_send.at[c], me + hop_b)

    def g_wait(dev, c):
        g_copy(new_buf.at[pl.ds(c * rows, rows)], dev, c, gy_send.at[0], partner).wait_recv()

    def local_copies(c):
        part = pl.ds(c * rows, rows)
        return [
            pltpu.make_async_copy(
                new_buf.at[part], gathered.at[pl.ds(me * shard + c * rows, rows)], g_local.at[c]
            ),
            pltpu.make_async_copy(m_buf.at[part], out_m.at[part], o_sem.at[c]),
            pltpu.make_async_copy(v_buf.at[part], out_v.at[part], o_sem.at[CHUNKS + c]),
        ]

    for c in range(CHUNKS):

        @pl.loop(0, rows // TILE)
        def _(b):
            at = pl.multiple_of(c * rows + b * TILE, TILE)
            matrix_id = (me * shard + at) // BLOCK
            decayed = jnp.where((matrix_id != 4) & (matrix_id < nmat - EMAT), 1.0, 0.0)
            part = pl.ds(at, TILE)
            new_w, new_m, new_v = update(
                summed[part, :] * factor, w_buf[part, :], m_buf[part, :], v_buf[part, :], decayed
            )
            m_buf[part, :] = new_m
            v_buf[part, :] = new_v
            new_buf[part, :] = new_w.astype(jnp.bfloat16)

        own_y(c).start()

        @pl.when(z < 3)
        def _():
            own_z(c, 2, 0).start()

        @pl.when(z > 0)
        def _():
            own_z(c, -2, 1).start()

        for copy in local_copies(c):
            copy.start()

    @pl.when(end)
    def _():
        for dst in late:
            a_copy(dst).start()

    for i in (2, 1, 0):
        for c in range(CHUNKS):

            def forward():
                g_wait(order[i] * 2 + y, c)

                @pl.when(mid)
                def _():
                    fwd_z(i, c).start()

                not_paired(i, c, lambda: fwd_y(i, c).start())

            forward()
            if i == 2:

                def pass_on():
                    g_wait(z * 2 + 1 - y, c)
                    fwd_p(c).start()

                if c < HALF:
                    pass_on()
                else:
                    pl.when(end)(pass_on)

    for i in range(4):
        for c in range(CHUNKS):
            if i < 3:
                g_wait(order[i] * 2 + 1 - y, c)
            elif c >= HALF:
                pl.when(mid)(lambda: g_wait(z * 2 + 1 - y, c))
    for n in range(total_chunks):
        not_paired(n // CHUNKS, n % CHUNKS, lambda: y_copy(n).wait_send())
    for i in range(3):
        for c in range(CHUNKS):
            z_copy(i, c).wait_send()
            not_paired(i, c, lambda: fwd_y(i, c).wait_send())
    for c in range(CHUNKS):
        if c < HALF:
            p_copy(c).wait_send()
            fwd_p(c).wait_send()
        else:
            pl.when(mid)(lambda: p_copy(c).wait_send())
            pl.when(end)(lambda: fwd_p(c).wait_send())
    for k in range(1, n_dp):
        dp_copy(k).wait_send()
        a_wait(k)
    for dst in middle:
        a_copy(dst).wait_send()

    @pl.when(end)
    def _():
        a_copy(far + y).wait_send()
        for dst in late:
            a_copy(dst).wait_send()

    @pl.when(mid)
    def _():
        for dst in early:
            a_copy(dst).wait_send()
        for k in range(2):
            r_copy(k).wait_send()
            f_copy(k).wait_send()

    a_own.wait()
    for k in range(1, n_mp):
        mp_copy(k).wait_send()
    for c in range(CHUNKS):
        own_y(c).wait_send()
        for copy in local_copies(c):
            copy.wait()

    @pl.when(z < 3)
    def _():
        for c in range(CHUNKS):
            own_z(c, 2, 0).wait_send()

    @pl.when(z > 0)
    def _():
        for c in range(CHUNKS):
            own_z(c, -2, 1).wait_send()

    @pl.when(mid)
    def _():
        for i in range(3):
            for c in range(CHUNKS):
                fwd_z(i, c).wait_send()


def finish_kernel(
    n_dp, most, nmat, owners, gathered, unpacked, m_in, v_in,
    out_w, owned, m_out, v_out, w_buf, fresh_buf, matrix_at, slot_at, w_sem, fresh_sem, state_sem
):
    me = lax.axis_index("dp")
    local = nmat // n_dp
    parts = gathered.shape[0] // PART

    state = [
        pltpu.make_async_copy(m_in, m_out, state_sem.at[0]),
        pltpu.make_async_copy(v_in, v_out, state_sem.at[1]),
    ]

    def w_copy(i):
        return pltpu.make_async_copy(
            w_buf.at[i % DEPTH], out_w.at[pl.ds(i * PART, PART)], w_sem.at[i % DEPTH]
        )

    def fresh_copy(j):
        return pltpu.make_async_copy(
            fresh_buf.at[j], owned.at[0, pl.ds(j * BLOCK, BLOCK)], fresh_sem.at[j]
        )

    def widen(i):
        if i >= DEPTH:
            w_copy(i - DEPTH).wait()

        @pl.loop(0, PART // TILE)
        def _(b):
            at = pl.multiple_of(b * TILE, TILE)
            w_buf[i % DEPTH, pl.ds(at, TILE), :] = gathered[pl.ds(i * PART + at, TILE), :].astype(
                jnp.float32
            )

        w_copy(i).start()

    def scan(src, kept):
        def one(k, carry):
            kept, here = carry
            g = src * local + k
            mine = (owners[g] == me).astype(jnp.int32)
            matrix_at[kept] = g
            slot_at[kept] = src * 2 + here
            return kept + mine, here + mine

        return lax.fori_loop(0, local, one, (kept, jnp.int32(0)))[0]

    def pick(j, count):
        @pl.when(j < count)
        def _():
            w_part = pl.ds(pl.multiple_of(matrix_at[j] * BLOCK, BLOCK), BLOCK)
            fresh = average_decay * unpacked[slot_at[j]].astype(jnp.float32) + (
                1.0 - average_decay
            ) * gathered[w_part, :].astype(jnp.float32)
            fresh_buf[j] = fresh.astype(jnp.bfloat16)

        @pl.when(j >= count)
        def _():
            fresh_buf[j] = jnp.zeros(fresh_buf.shape[1:], jnp.bfloat16)

        fresh_copy(j).start()

    for i in range(DEPTH):
        widen(i)
    for copy in state:
        copy.start()
    count = lax.fori_loop(0, n_dp, scan, jnp.int32(0))
    for j in range(most):
        pick(j, count)
    for i in range(DEPTH, parts):
        widen(i)
    for i in range(parts - DEPTH, parts):
        w_copy(i).wait()
    for j in range(most):
        fresh_copy(j).wait()
    for copy in state:
        copy.wait()


def grid_shards(n_dp, n_mp, limit, grads, weights, moment1, moment2, average, owners):
    shard, width = weights.shape
    local = shard // BLOCK
    most = local + local // 2
    nmat = owners.shape[0]
    total_rows = grads.shape[1]
    owner_col = pltpu.with_memory_space_constraint(owners[:, 0], pltpu.HBM)
    any_spec = pl.BlockSpec(memory_space=pl.ANY)
    smem_spec = pl.BlockSpec(memory_space=pltpu.SMEM)
    bf16, f32 = jnp.bfloat16, jnp.float32
    dma = pltpu.SemaphoreType.DMA

    average = average.reshape(local, BLOCK, width)
    grads, weights, moment1, moment2, average = (
        pltpu.with_memory_space_constraint(a, pltpu.HBM)
        for a in (grads, weights, moment1, moment2, average)
    )
    gathered, new_m, new_v, unpacked = pl.pallas_call(
        functools.partial(step_kernel, n_dp, n_mp, limit, nmat),
        out_shape=(
            pltpu.VMEM((total_rows, width), bf16),
            pltpu.VMEM((shard, width), f32),
            pltpu.VMEM((shard, width), f32),
            pltpu.VMEM((n_dp * 2, BLOCK, width), bf16),
        ),
        in_specs=[smem_spec] + [any_spec] * 5,
        out_specs=(any_spec,) * 4,
        scratch_shapes=[
            pltpu.VMEM((4, shard, width), bf16),
            pltpu.VMEM((4, shard, width), bf16),
            pltpu.VMEM((5, shard, width), bf16),
            pltpu.VMEM((shard, width), f32),
            pltpu.VMEM((shard, width), f32),
            pltpu.VMEM((shard, width), f32),
            pltpu.VMEM((shard, width), f32),
            pltpu.VMEM((shard, width), bf16),
            pltpu.VMEM((n_dp, 8, width), f32),
            pltpu.VMEM((n_mp, 8, width), f32),
            pltpu.VMEM((shard, width), bf16),
            pltpu.VMEM((shard, width), bf16),
            pltpu.VMEM((local, BLOCK, width), bf16),
            pltpu.VMEM((n_dp * 2, BLOCK, width), bf16),
            pltpu.VMEM((4, BLOCK, width), bf16),
            dma((9,)),
            dma((4 * CHUNKS,)),
            dma((4 * CHUNKS,)),
            dma((3 * CHUNKS,)),
            dma((5 * CHUNKS,)),
            dma((n_dp,)),
            dma((n_dp,)),
            dma((n_mp,)),
            dma((n_mp,)),
            dma((n_dp,)),
            dma((n_dp,)),
            dma((1,)),
            dma((2,)),
            dma((2,)),
            dma((2,)),
            dma((4 * CHUNKS,)),
            dma((2 * CHUNKS,)),
            dma((3 * CHUNKS,)),
            dma((n_dp * CHUNKS,)),
            dma((CHUNKS,)),
            dma((2 * CHUNKS,)),
            dma((CHUNKS,)),
            dma((CHUNKS,)),
            dma((CHUNKS,)),
        ],
        compiler_params=pltpu.CompilerParams(
            collective_id=0, has_side_effects=True, vmem_limit_bytes=32 * 2**20
        ),
    )(owner_col, grads, weights, moment1, moment2, average)

    gathered, new_m, new_v, unpacked = (
        pltpu.with_memory_space_constraint(a, pltpu.VMEM) for a in (gathered, new_m, new_v, unpacked)
    )
    vmem_spec = pl.BlockSpec(memory_space=pltpu.VMEM)
    new_full, owned, new_m, new_v = pl.pallas_call(
        functools.partial(finish_kernel, n_dp, most, nmat),
        out_shape=(
            jax.ShapeDtypeStruct((total_rows, width), f32),
            jax.ShapeDtypeStruct((1, most * BLOCK, width), bf16),
            jax.ShapeDtypeStruct((shard, width), f32),
            jax.ShapeDtypeStruct((shard, width), f32),
        ),
        in_specs=[smem_spec, vmem_spec, vmem_spec, any_spec, any_spec],
        out_specs=(any_spec,) * 4,
        scratch_shapes=[
            pltpu.VMEM((DEPTH, PART, width), f32),
            pltpu.VMEM((most, BLOCK, width), bf16),
            pltpu.SMEM((most + 1,), jnp.int32),
            pltpu.SMEM((most + 1,), jnp.int32),
            dma((DEPTH,)),
            dma((most,)),
            dma((2,)),
        ],
        compiler_params=pltpu.CompilerParams(vmem_limit_bytes=16 * 2**20),
    )(owner_col, gathered, unpacked, new_m, new_v)
    return (new_full, new_m, new_v, owned)


def solution(mesh):
    n_dp, n_mp = mesh.shape["dp"], mesh.shape["mp"]

    def step(grads, weights, moment1, moment2, average, owners):
        limit = float(weights.shape[0] * weights.shape[1]) ** 0.5
        if n_dp == 8:
            body = functools.partial(grid_shards, n_dp, n_mp, limit)
        else:
            body = functools.partial(plain_shards, limit)
        placed = (P("dp", None, "mp"), P("dp", "mp"), P("dp", "mp"), P("dp", "mp"), P("dp", "mp"), P())
        return jax.shard_map(
            body,
            mesh=mesh,
            in_specs=placed,
            out_specs=(P(None, "mp"), P("dp", "mp"), P("dp", "mp"), P("dp", None, "mp")),
            check_vma=False,
        )(grads, weights, moment1, moment2, average, owners)

    return step
```

```python
import functools

import jax
import jax.numpy as jnp
from jax import lax
from jax.experimental import pallas as pl
from jax.experimental.pallas import tpu as pltpu
from jax.sharding import PartitionSpec as P

BLOCK = 256
EMAT = 32
MESH = pl.DeviceIdType.MESH


learning = 0.05
beta_one = 0.9
beta_two = 0.95
epsilon = 1e-08
weight_decay = 0.1
average_decay = 0.9
step_count = 10


def update(clipped, weights, moment1, moment2, decayed):
    new_m = beta_one * moment1 + (1.0 - beta_one) * clipped
    new_v = beta_two * moment2 + (1.0 - beta_two) * clipped * clipped
    v_hat = new_v * (1.0 / (1.0 - beta_two**step_count))
    rate = learning / (1.0 - beta_one**step_count)
    new_w = weights * (1.0 - learning * weight_decay * decayed) - rate * new_m / (
        jnp.sqrt(v_hat) + epsilon
    )
    return (new_w, new_m, new_v)


def pick_owned(fresh_full, owner_col, owner_id, most, nmat):
    flags = owner_col == owner_id
    ids = jnp.arange(nmat, dtype=jnp.int32)
    position = jnp.sum((flags[None, :] & (ids[None, :] <= ids[:, None])).astype(jnp.int32), axis=1) - 1
    slots = jnp.arange(most, dtype=jnp.int32)
    select = (flags[None, :] & (position[None, :] == slots[:, None])).astype(jnp.bfloat16)
    stacked = fresh_full.reshape(nmat, -1)
    picked = jnp.dot(select, stacked, preferred_element_type=jnp.float32)
    return picked.astype(jnp.bfloat16).reshape(1, most * BLOCK, -1)


def plain_shards(limit, grads, weights, moment1, moment2, average, owners):
    shard_rows = weights.shape[0]
    local_count = shard_rows // BLOCK
    most = local_count + local_count // 2
    nmat = owners.shape[0]
    my_index = lax.axis_index("dp")
    summed = lax.psum_scatter(grads[0], "dp", scatter_dimension=0, tiled=True).astype(jnp.float32)
    total = lax.psum(jnp.sum(summed * summed), ("dp", "mp"))
    factor = jnp.minimum(1.0, limit / (jnp.sqrt(total) + 1e-06))
    row_ids = my_index * shard_rows + jnp.arange(shard_rows, dtype=jnp.int32)
    matrix_id = row_ids // BLOCK
    decayed = ((matrix_id != 4) & (matrix_id < nmat - EMAT)).astype(jnp.float32)[:, None]
    new_w, new_m, new_v = update(summed * factor, weights, moment1, moment2, decayed)
    new_full = lax.all_gather(new_w, "dp", axis=0, tiled=True)
    fresh = (average_decay * average.astype(jnp.float32) + (1.0 - average_decay) * new_w).astype(
        jnp.bfloat16
    )
    fresh_full = lax.all_gather(fresh, "dp", axis=0, tiled=True)
    owned = pick_owned(fresh_full, owners[:, 0], my_index, most, nmat)
    return (new_full, new_m, new_v, owned)


CHUNKS = 8
HALF = CHUNKS // 2
PART = 1024
DEPTH = 4
DIRECT_AT = 2
RELAY_AT = 12
PAIR_AT = 10
KEEP = 2
WINDOW = 10
TILE = 64


def step_kernel(
    n_dp, n_mp, limit, nmat,
    owners, grads, weights, moment1, moment2, average,
    gathered, out_m, out_v, unpacked,
    own, from_y, from_z, summed, w_buf, m_buf, v_buf, new_buf, part_dp, part_mp, other, from_p,
    kept, packed, relay,
    load_sem, y_send, y_recv, z_send, z_recv, dp_send, dp_recv, mp_send, mp_recv,
    a_send, a_recv, a_local, r_recv, gy_send, gz_send, g_recv, g_rest, g_local, o_sem, p_recv,
):
    me = lax.axis_index("dp")
    col = lax.axis_index("mp")
    z, y = me // 2, me % 2
    partner = me + 1 - 2 * y
    shard = weights.shape[0]
    rows = shard // CHUNKS
    width = weights.shape[1]
    mid = (z == 1) | (z == 2)
    end = (z == 0) | (z == 3)

    barrier = pltpu.get_barrier_semaphore()
    for k in range(1, n_dp):
        pl.semaphore_signal(
            barrier, inc=1, device_id=(lax.rem(me + k, n_dp), col), device_id_type=MESH
        )
    for k in range(1, n_mp):
        pl.semaphore_signal(
            barrier, inc=1, device_id=(me, lax.rem(col + k, n_mp)), device_id_type=MESH
        )

    order = [3 * (1 - z // 2), (2 + 3 * z) % 5, 1 + z % 2, z]
    hop_a = 2 * (1 - 2 * (z // 2))
    hop_b = 2 * (1 - 2 * (z % 2))
    hops = [hop_a, hop_b, hop_a]
    pair = z + 1 - 2 * (z % 2)

    loads = []
    for i in range(4):
        t = order[i]
        loads.append(
            pltpu.make_async_copy(
                grads.at[0, pl.ds((t * 2 + y) * shard, shard)], own.at[t], load_sem.at[i]
            )
        )
        loads[-1].start()
    state = []
    for i, (src, dst) in enumerate(((weights, w_buf), (moment1, m_buf), (moment2, v_buf))):
        state.append(pltpu.make_async_copy(src, dst, load_sem.at[4 + i]))

    other_load = pltpu.make_async_copy(
        grads.at[0, pl.ds((z * 2 + 1 - y) * shard, shard)], other, load_sem.at[7]
    )
    other_load.start()
    kept_load = pltpu.make_async_copy(average, kept, load_sem.at[8])
    kept_load.start()

    pl.semaphore_wait(barrier, n_dp - 1 + n_mp - 1)

    def not_paired(i, c, fn):
        if i == 1:
            pl.when(end)(fn)
        elif c < HALF and i == 2:
            pl.when(mid)(fn)
        else:
            fn()

    def p_copy(c):
        return pltpu.make_async_remote_copy(
            src_ref=grads.at[0, pl.ds((pair * 2 + 1 - y) * shard + c * rows, rows)],
            dst_ref=from_p.at[pl.ds(c * rows, rows)],
            send_sem=z_send,
            recv_sem=p_recv.at[c // HALF],
            device_id=(me + hop_b, col),
            device_id_type=MESH,
        )

    def y_copy(n):
        t, c = order[n // CHUNKS], n % CHUNKS
        if n // CHUNKS == 3:
            src = other.at[pl.ds(c * rows, rows)]
        else:
            src = grads.at[0, pl.ds((t * 2 + 1 - y) * shard + c * rows, rows)]
        return pltpu.make_async_remote_copy(
            src_ref=src,
            dst_ref=from_y.at[t, pl.ds(c * rows, rows)],
            send_sem=y_send,
            recv_sem=y_recv.at[n],
            device_id=(partner, col),
            device_id_type=MESH,
        )

    def z_copy(i, c):
        t = order[i]
        slot = t if i < 2 else t + (4 - t) * (z // 2)
        return pltpu.make_async_remote_copy(
            src_ref=own.at[t, pl.ds(c * rows, rows)],
            dst_ref=from_z.at[slot, pl.ds(c * rows, rows)],
            send_sem=z_send,
            recv_sem=z_recv.at[slot * CHUNKS + c],
            device_id=(me + hops[i], col),
            device_id_type=MESH,
        )

    def z_wait(slot, c):
        pltpu.make_async_remote_copy(
            src_ref=own.at[0, pl.ds(c * rows, rows)],
            dst_ref=from_z.at[slot, pl.ds(c * rows, rows)],
            send_sem=z_send,
            recv_sem=z_recv.at[slot * CHUNKS + c],
            device_id=(partner, col),
            device_id_type=MESH,
        ).wait_recv()

    def f32(ref, at, start):
        return ref[at, pl.ds(start, TILE), :].astype(jnp.float32)

    slots = 2
    far = (3 - z) * 2
    local = kept.shape[0]

    def pack():
        for dst in range(n_dp):
            first, second, count = jnp.int32(0), jnp.int32(0), jnp.int32(0)
            for k in range(local):
                hit = (owners[me * local + k] == dst).astype(jnp.int32)
                first += hit * (count == 0).astype(jnp.int32) * k
                second += hit * (count == 1).astype(jnp.int32) * k
                count += hit
            packed[dst * slots] = kept[first]
            packed[dst * slots + 1] = kept[second]

    def a_send_copy(src_ref, src, dst):
        return pltpu.make_async_remote_copy(
            src_ref=src_ref,
            dst_ref=unpacked.at[pl.ds(src * slots, slots)],
            send_sem=a_send,
            recv_sem=a_recv,
            device_id=(dst, col),
            device_id_type=MESH,
        )

    def a_copy(dst):
        return a_send_copy(packed.at[pl.ds(dst * slots, slots)], me, dst)

    def r_copy(k):
        dst = 6 * k + 1 - y
        return pltpu.make_async_remote_copy(
            src_ref=packed.at[pl.ds(dst * slots, slots)],
            dst_ref=relay.at[pl.ds(k * slots, slots)],
            send_sem=a_send,
            recv_sem=r_recv.at[k],
            device_id=(partner, col),
            device_id_type=MESH,
        )

    def f_copy(k):
        return a_send_copy(relay.at[pl.ds(k * slots, slots)], partner, 6 * k + y)

    def whole(ref, count, send_sem, recv_sem):
        part = ref.at[pl.ds(0, count)]
        return pltpu.make_async_remote_copy(
            src_ref=part,
            dst_ref=part,
            send_sem=send_sem,
            recv_sem=recv_sem,
            device_id=(partner, col),
            device_id_type=MESH,
        )

    early = [y, 6 + y, far + y]
    middle = [partner, far + 1 - y]
    late = [2, 3, 4, 5]

    total_chunks = 4 * CHUNKS
    def y_start(n):
        if n < total_chunks:
            not_paired(n // CHUNKS, n % CHUNKS, lambda: y_copy(n).start())

    for n in range(WINDOW):
        y_start(n)
    for c in range(HALF):
        p_copy(c).start()
    kept_load.wait()
    pack()

    @pl.when(mid)
    def _():
        for c in range(HALF, CHUNKS):
            p_copy(c).start()
        for k in range(2):
            r_copy(k).start()

    for s in state:
        s.start()

    for n in range(3 * CHUNKS):
        i, c = n // CHUNKS, n % CHUNKS
        t = order[i]
        if c == 0:
            loads[i].wait()
        if n == DIRECT_AT:

            @pl.when(mid)
            def _():
                for dst in early:
                    a_copy(dst).start()

        if n == RELAY_AT:

            @pl.when(mid)
            def _():
                for k in range(2):
                    r_copy(k).wait_recv()
                    f_copy(k).start()

        if n == PAIR_AT:
            other_load.wait()
        k = n - PAIR_AT
        if 0 <= k < CHUNKS:

            def join():
                if k % HALF == 0:
                    whole(from_p, HALF * rows, z_send, p_recv.at[k // HALF]).wait_recv()

                @pl.loop(0, rows // TILE)
                def _(b):
                    part = pl.ds(pl.multiple_of(k * rows + b * TILE, TILE), TILE)
                    val = other[part, :].astype(jnp.float32) + from_p[part, :].astype(jnp.float32)
                    other[part, :] = val.astype(jnp.bfloat16)

            if k < HALF:
                join()
            else:
                pl.when(end)(join)

        not_paired(i, c, lambda: y_copy(n).wait_recv())
        y_start(n + WINDOW)

        def add(with_y, with_z):
            if with_z:
                z_wait(t, c)

            @pl.loop(0, rows // TILE)
            def _(b):
                at = pl.multiple_of(c * rows + b * TILE, TILE)
                val = f32(own, t, at)
                if with_y:
                    val = val + f32(from_y, t, at)
                if with_z:
                    val = val + f32(from_z, t, at)
                own[t, pl.ds(at, TILE), :] = val.astype(jnp.bfloat16)

        paired_mid = i == 1
        paired_end = c < HALF and i == 2
        pl.when(mid)(functools.partial(add, not paired_mid, True))
        if not paired_end:
            pl.when(end)(functools.partial(add, True, False))
        z_copy(i, c).start()

    loads[3].wait()
    part_dp[me] = jnp.zeros((8, width), jnp.float32)
    for c in range(CHUNKS):
        n = 3 * CHUNKS + c
        y_copy(n).wait_recv()
        y_start(n + WINDOW)
        z_wait(z, c)

        def keep(at, val):
            summed[pl.ds(at, TILE), :] = val
            part_dp[me] += jnp.sum((val * val).reshape(TILE // 8, 8, width), axis=0)

        @pl.when(mid)
        def _():
            z_wait(4, c)

            @pl.loop(0, rows // TILE)
            def _(b):
                at = pl.multiple_of(c * rows + b * TILE, TILE)
                keep(at, f32(own, z, at) + f32(from_y, z, at) + f32(from_z, z, at) + f32(from_z, 4, at))

        @pl.when(end)
        def _():
            @pl.loop(0, rows // TILE)
            def _(b):
                at = pl.multiple_of(c * rows + b * TILE, TILE)
                keep(at, f32(own, z, at) + f32(from_y, z, at) + f32(from_z, z, at))

    def dp_copy(k):
        return pltpu.make_async_remote_copy(
            src_ref=part_dp.at[me],
            dst_ref=part_dp.at[me],
            send_sem=dp_send,
            recv_sem=dp_recv,
            device_id=(lax.rem(me + k, n_dp), col),
            device_id_type=MESH,
        )

    def mp_copy(k):
        return pltpu.make_async_remote_copy(
            src_ref=part_mp.at[col],
            dst_ref=part_mp.at[col],
            send_sem=mp_send,
            recv_sem=mp_recv,
            device_id=(me, lax.rem(col + k, n_mp)),
            device_id_type=MESH,
        )

    all_dp = whole(part_dp, n_dp - 1, dp_send, dp_recv)
    all_mp = whole(part_mp, n_mp - 1, mp_send, mp_recv)

    for k in range(1, n_dp):
        dp_copy(k).start()
    a_own = pltpu.make_async_copy(
        packed.at[pl.ds(me * slots, slots)], unpacked.at[pl.ds(me * slots, slots)], a_local
    )
    a_own.start()
    all_dp.wait_recv()
    group = part_dp[0]
    for k in range(1, n_dp):
        group = group + part_dp[k]
    part_mp[col] = group
    for k in range(1, n_mp):
        mp_copy(k).start()
    for dst in middle:
        a_copy(dst).start()

    @pl.when(end)
    def _():
        a_copy(far + y).start()

    for s in state:
        s.wait()
    all_mp.wait_recv()
    everything = part_mp[0]
    for k in range(1, n_mp):
        everything = everything + part_mp[k]
    total = jnp.sum(everything, axis=(0, 1), keepdims=True)
    factor = jnp.minimum(1.0, limit / (jnp.sqrt(total) + 1e-06))

    def g_copy(src_ref, dev, c, send_sem, recv_sem, target):
        return pltpu.make_async_remote_copy(
            src_ref=src_ref,
            dst_ref=gathered.at[pl.ds(dev * shard + c * rows, rows)],
            send_sem=send_sem,
            recv_sem=recv_sem,
            device_id=(target, col),
            device_id_type=MESH,
        )

    def held(dev, c):
        return gathered.at[pl.ds(dev * shard + c * rows, rows)]

    def step_sem(plane, c):
        return g_recv.at[plane * CHUNKS + c]

    def own_y(c):
        return g_copy(new_buf.at[pl.ds(c * rows, rows)], me, c, gy_send, step_sem(z, c), partner)

    def own_z(c, hop):
        return g_copy(new_buf.at[pl.ds(c * rows, rows)], me, c, gz_send, step_sem(z, c), me + hop)

    def fwd_y(i, c):
        dev = order[i] * 2 + y
        return g_copy(held(dev, c), dev, c, gy_send, g_rest, partner)

    def fwd_z(i, c):
        dev = order[i] * 2 + y
        return g_copy(held(dev, c), dev, c, gz_send, step_sem(order[i], c), me - hops[i])

    def fwd_p(c):
        dev = z * 2 + 1 - y
        return g_copy(held(dev, c), dev, c, gz_send, g_rest, me + hop_b)

    def g_wait(plane, side, c):
        g_copy(
            new_buf.at[pl.ds(c * rows, rows)], plane * 2 + side, c, gy_send, step_sem(plane, c), partner
        ).wait_recv()

    def local_copies(c):
        part = pl.ds(c * rows, rows)
        return [
            pltpu.make_async_copy(
                new_buf.at[part], gathered.at[pl.ds(me * shard + c * rows, rows)], g_local
            ),
            pltpu.make_async_copy(m_buf.at[part], out_m.at[part], o_sem.at[0]),
            pltpu.make_async_copy(v_buf.at[part], out_v.at[part], o_sem.at[1]),
        ]

    for c in range(CHUNKS):

        @pl.loop(0, rows // TILE)
        def _(b):
            at = pl.multiple_of(c * rows + b * TILE, TILE)
            matrix_id = (me * shard + at) // BLOCK
            decayed = jnp.where((matrix_id != 4) & (matrix_id < nmat - EMAT), 1.0, 0.0)
            part = pl.ds(at, TILE)
            new_w, new_m, new_v = update(
                summed[part, :] * factor, w_buf[part, :], m_buf[part, :], v_buf[part, :], decayed
            )
            m_buf[part, :] = new_m
            v_buf[part, :] = new_v
            new_buf[part, :] = new_w.astype(jnp.bfloat16)

        own_y(c).start()

        @pl.when(z < 3)
        def _():
            own_z(c, 2).start()

        @pl.when(z > 0)
        def _():
            own_z(c, -2).start()

        for copy in local_copies(c):
            copy.start()

    @pl.when(end)
    def _():
        for dst in late:
            a_copy(dst).start()

    for i in (2, 1, 0):
        for c in range(CHUNKS):

            def forward():
                g_wait(order[i], y, c)

                @pl.when(mid)
                def _():
                    fwd_z(i, c).start()

                not_paired(i, c, lambda: fwd_y(i, c).start())

            forward()
            if i == 2:

                def pass_on():
                    g_wait(z, 1 - y, c)
                    fwd_p(c).start()

                if c < HALF - KEEP:
                    pass_on()
                else:
                    pl.when(end)(pass_on)

    @pl.when(mid)
    def _():
        for c in range(HALF - KEEP, HALF):
            g_wait(z, 1 - y, c)
            fwd_p(c).start()

    @pl.when(mid)
    def _():
        for c in range(HALF, CHUNKS):
            g_wait(z, 1 - y, c)

    def drain(ref, count, sem):
        whole(ref, count, sem, g_rest).wait_send()

    @pl.when(end)
    def _():
        drain(gathered, (4 * CHUNKS - HALF) * rows, y_send)
        drain(gathered, (3 * CHUNKS + HALF) * rows, z_send)
        drain(gathered, (4 * CHUNKS - HALF) * rows, gy_send)
        drain(gathered, 2 * CHUNKS * rows, gz_send)
        drain(unpacked, 7 * slots, a_send)

    @pl.when(mid)
    def _():
        drain(gathered, 3 * CHUNKS * rows, y_send)
        drain(gathered, 4 * CHUNKS * rows, z_send)
        drain(gathered, 3 * CHUNKS * rows, gy_send)
        drain(gathered, (5 * CHUNKS + HALF) * rows, gz_send)
        drain(gathered, 9 * slots * BLOCK, a_send)

    all_dp.wait_send()
    all_mp.wait_send()
    a_own.wait()
    pltpu.make_async_copy(new_buf, gathered.at[pl.ds(me * shard, shard)], g_local).wait()
    pltpu.make_async_copy(m_buf, out_m, o_sem.at[0]).wait()
    pltpu.make_async_copy(v_buf, out_v, o_sem.at[1]).wait()
    whole(unpacked, (n_dp - 1) * slots, a_send, a_recv).wait_recv()
    whole(gathered, 3 * CHUNKS * rows, gz_send, g_rest).wait_recv()


def finish_kernel(
    n_dp, most, nmat, owners, gathered, unpacked, m_in, v_in,
    out_w, owned, m_out, v_out, w_buf, fresh_buf, matrix_at, slot_at, w_sem, fresh_sem, state_sem
):
    me = lax.axis_index("dp")
    local = nmat // n_dp
    parts = gathered.shape[0] // PART

    state = [
        pltpu.make_async_copy(m_in, m_out, state_sem.at[0]),
        pltpu.make_async_copy(v_in, v_out, state_sem.at[1]),
    ]

    def w_copy(i):
        return pltpu.make_async_copy(
            w_buf.at[i % DEPTH], out_w.at[pl.ds(i * PART, PART)], w_sem.at[i % DEPTH]
        )

    def fresh_copy(j):
        return pltpu.make_async_copy(
            fresh_buf.at[j], owned.at[0, pl.ds(j * BLOCK, BLOCK)], fresh_sem.at[j]
        )

    def widen(i):
        if i >= DEPTH:
            w_copy(i - DEPTH).wait()

        @pl.loop(0, PART // TILE)
        def _(b):
            at = pl.multiple_of(b * TILE, TILE)
            w_buf[i % DEPTH, pl.ds(at, TILE), :] = gathered[pl.ds(i * PART + at, TILE), :].astype(
                jnp.float32
            )

        w_copy(i).start()

    def scan(src, kept):
        def one(k, carry):
            kept, here = carry
            g = src * local + k
            mine = (owners[g] == me).astype(jnp.int32)
            matrix_at[kept] = g
            slot_at[kept] = src * 2 + here
            return kept + mine, here + mine

        return lax.fori_loop(0, local, one, (kept, jnp.int32(0)))[0]

    def pick(j, count):
        @pl.when(j < count)
        def _():
            w_part = pl.ds(pl.multiple_of(matrix_at[j] * BLOCK, BLOCK), BLOCK)
            fresh = average_decay * unpacked[slot_at[j]].astype(jnp.float32) + (
                1.0 - average_decay
            ) * gathered[w_part, :].astype(jnp.float32)
            fresh_buf[j] = fresh.astype(jnp.bfloat16)

        @pl.when(j >= count)
        def _():
            fresh_buf[j] = jnp.zeros(fresh_buf.shape[1:], jnp.bfloat16)

        fresh_copy(j).start()

    for i in range(DEPTH):
        widen(i)
    for copy in state:
        copy.start()
    count = lax.fori_loop(0, n_dp, scan, jnp.int32(0))
    for j in range(most):
        pick(j, count)
    for i in range(DEPTH, parts):
        widen(i)
    for i in range(parts - DEPTH, parts):
        w_copy(i).wait()
    for j in range(most):
        fresh_copy(j).wait()
    for copy in state:
        copy.wait()


def grid_shards(n_dp, n_mp, limit, grads, weights, moment1, moment2, average, owners):
    shard, width = weights.shape
    local = shard // BLOCK
    most = local + local // 2
    nmat = owners.shape[0]
    total_rows = grads.shape[1]
    owner_col = pltpu.with_memory_space_constraint(owners[:, 0], pltpu.HBM)
    any_spec = pl.BlockSpec(memory_space=pl.ANY)
    smem_spec = pl.BlockSpec(memory_space=pltpu.SMEM)
    bf16, f32 = jnp.bfloat16, jnp.float32
    dma = pltpu.SemaphoreType.DMA

    average = average.reshape(local, BLOCK, width)
    grads, weights, moment1, moment2, average = (
        pltpu.with_memory_space_constraint(a, pltpu.HBM)
        for a in (grads, weights, moment1, moment2, average)
    )
    gathered, new_m, new_v, unpacked = pl.pallas_call(
        functools.partial(step_kernel, n_dp, n_mp, limit, nmat),
        out_shape=(
            pltpu.VMEM((total_rows, width), bf16),
            pltpu.VMEM((shard, width), f32),
            pltpu.VMEM((shard, width), f32),
            pltpu.VMEM((n_dp * 2, BLOCK, width), bf16),
        ),
        in_specs=[smem_spec] + [any_spec] * 5,
        out_specs=(any_spec,) * 4,
        scratch_shapes=[
            pltpu.VMEM((4, shard, width), bf16),
            pltpu.VMEM((4, shard, width), bf16),
            pltpu.VMEM((5, shard, width), bf16),
            pltpu.VMEM((shard, width), f32),
            pltpu.VMEM((shard, width), f32),
            pltpu.VMEM((shard, width), f32),
            pltpu.VMEM((shard, width), f32),
            pltpu.VMEM((shard, width), bf16),
            pltpu.VMEM((n_dp, 8, width), f32),
            pltpu.VMEM((n_mp, 8, width), f32),
            pltpu.VMEM((shard, width), bf16),
            pltpu.VMEM((shard, width), bf16),
            pltpu.VMEM((local, BLOCK, width), bf16),
            pltpu.VMEM((n_dp * 2, BLOCK, width), bf16),
            pltpu.VMEM((4, BLOCK, width), bf16),
            dma((9,)),
            dma,
            dma((4 * CHUNKS,)),
            dma,
            dma((5 * CHUNKS,)),
            dma,
            dma,
            dma,
            dma,
            dma,
            dma,
            dma,
            dma((2,)),
            dma,
            dma,
            dma((4 * CHUNKS,)),
            dma,
            dma,
            dma((2,)),
            dma((2,)),
        ],
        compiler_params=pltpu.CompilerParams(
            collective_id=0, has_side_effects=True, vmem_limit_bytes=32 * 2**20
        ),
    )(owner_col, grads, weights, moment1, moment2, average)

    gathered, new_m, new_v, unpacked = (
        pltpu.with_memory_space_constraint(a, pltpu.VMEM) for a in (gathered, new_m, new_v, unpacked)
    )
    vmem_spec = pl.BlockSpec(memory_space=pltpu.VMEM)
    new_full, owned, new_m, new_v = pl.pallas_call(
        functools.partial(finish_kernel, n_dp, most, nmat),
        out_shape=(
            jax.ShapeDtypeStruct((total_rows, width), f32),
            jax.ShapeDtypeStruct((1, most * BLOCK, width), bf16),
            jax.ShapeDtypeStruct((shard, width), f32),
            jax.ShapeDtypeStruct((shard, width), f32),
        ),
        in_specs=[smem_spec, vmem_spec, vmem_spec, any_spec, any_spec],
        out_specs=(any_spec,) * 4,
        scratch_shapes=[
            pltpu.VMEM((DEPTH, PART, width), f32),
            pltpu.VMEM((most, BLOCK, width), bf16),
            pltpu.SMEM((most + 1,), jnp.int32),
            pltpu.SMEM((most + 1,), jnp.int32),
            dma((DEPTH,)),
            dma((most,)),
            dma((2,)),
        ],
        compiler_params=pltpu.CompilerParams(vmem_limit_bytes=16 * 2**20),
    )(owner_col, gathered, unpacked, new_m, new_v)
    return (new_full, new_m, new_v, owned)


def solution(mesh):
    n_dp, n_mp = mesh.shape["dp"], mesh.shape["mp"]

    def step(grads, weights, moment1, moment2, average, owners):
        limit = float(weights.shape[0] * weights.shape[1]) ** 0.5
        if n_dp == 8:
            body = functools.partial(grid_shards, n_dp, n_mp, limit)
        else:
            body = functools.partial(plain_shards, limit)
        placed = (P("dp", None, "mp"), P("dp", "mp"), P("dp", "mp"), P("dp", "mp"), P("dp", "mp"), P())
        return jax.shard_map(
            body,
            mesh=mesh,
            in_specs=placed,
            out_specs=(P(None, "mp"), P("dp", "mp"), P("dp", "mp"), P("dp", None, "mp")),
            check_vma=False,
        )(grads, weights, moment1, moment2, average, owners)

    return step
```

```python
import functools

import jax
import jax.numpy as jnp
from jax import lax
from jax.experimental import pallas as pl
from jax.experimental.pallas import tpu as pltpu
from jax.sharding import PartitionSpec as P

BLOCK = 256
EMAT = 32
MESH = pl.DeviceIdType.MESH


learning = 0.05
beta_one = 0.9
beta_two = 0.95
epsilon = 1e-08
weight_decay = 0.1
average_decay = 0.9
step_count = 10


def update(clipped, weights, moment1, moment2, decayed):
    new_m = beta_one * moment1 + (1.0 - beta_one) * clipped
    new_v = beta_two * moment2 + (1.0 - beta_two) * clipped * clipped
    v_hat = new_v * (1.0 / (1.0 - beta_two**step_count))
    rate = learning / (1.0 - beta_one**step_count)
    new_w = weights * (1.0 - learning * weight_decay * decayed) - rate * new_m / (
        jnp.sqrt(v_hat) + epsilon
    )
    return (new_w, new_m, new_v)


def pick_owned(fresh_full, owner_col, owner_id, most, nmat):
    flags = owner_col == owner_id
    ids = jnp.arange(nmat, dtype=jnp.int32)
    position = jnp.sum((flags[None, :] & (ids[None, :] <= ids[:, None])).astype(jnp.int32), axis=1) - 1
    slots = jnp.arange(most, dtype=jnp.int32)
    select = (flags[None, :] & (position[None, :] == slots[:, None])).astype(jnp.bfloat16)
    stacked = fresh_full.reshape(nmat, -1)
    picked = jnp.dot(select, stacked, preferred_element_type=jnp.float32)
    return picked.astype(jnp.bfloat16).reshape(1, most * BLOCK, -1)


def plain_shards(limit, grads, weights, moment1, moment2, average, owners):
    shard_rows = weights.shape[0]
    local_count = shard_rows // BLOCK
    most = local_count + local_count // 2
    nmat = owners.shape[0]
    my_index = lax.axis_index("dp")
    summed = lax.psum_scatter(grads[0], "dp", scatter_dimension=0, tiled=True).astype(jnp.float32)
    total = lax.psum(jnp.sum(summed * summed), ("dp", "mp"))
    factor = jnp.minimum(1.0, limit / (jnp.sqrt(total) + 1e-06))
    row_ids = my_index * shard_rows + jnp.arange(shard_rows, dtype=jnp.int32)
    matrix_id = row_ids // BLOCK
    decayed = ((matrix_id != 4) & (matrix_id < nmat - EMAT)).astype(jnp.float32)[:, None]
    new_w, new_m, new_v = update(summed * factor, weights, moment1, moment2, decayed)
    new_full = lax.all_gather(new_w, "dp", axis=0, tiled=True)
    fresh = (average_decay * average.astype(jnp.float32) + (1.0 - average_decay) * new_w).astype(
        jnp.bfloat16
    )
    fresh_full = lax.all_gather(fresh, "dp", axis=0, tiled=True)
    owned = pick_owned(fresh_full, owners[:, 0], my_index, most, nmat)
    return (new_full, new_m, new_v, owned)


CHUNKS = 8
HALF = CHUNKS // 2
PART = 1024
DEPTH = 4
DIRECT_AT = 2
RELAY_AT = 12
PAIR_AT = 10
KEEP = 2
SPLIT = 3
CROSS = (0, 4)
PASS_AT = 2
WINDOW = 10
TILE = 64


def step_kernel(
    n_dp, n_mp, limit, nmat,
    owners, grads, weights, moment1, moment2, average,
    gathered, out_m, out_v, unpacked,
    own, from_y, from_z, summed, w_buf, m_buf, v_buf, new_buf, part_dp, part_mp, other, from_p,
    kept, packed, relay,
    load_sem, y_send, y_recv, z_send, z_recv, dp_send, dp_recv, mp_send, mp_recv,
    a_send, a_recv, a_local, r_recv, gy_send, gz_send, g_rest, g_local, o_sem, p_recv,
):
    me = lax.axis_index("dp")
    col = lax.axis_index("mp")
    z, y = me // 2, me % 2
    partner = me + 1 - 2 * y
    shard = weights.shape[0]
    rows = shard // CHUNKS
    width = weights.shape[1]
    mid = (z == 1) | (z == 2)
    end = (z == 0) | (z == 3)

    barrier = pltpu.get_barrier_semaphore()
    for k in range(1, n_dp):
        pl.semaphore_signal(
            barrier, inc=1, device_id=(lax.rem(me + k, n_dp), col), device_id_type=MESH
        )
    for k in range(1, n_mp):
        pl.semaphore_signal(
            barrier, inc=1, device_id=(me, lax.rem(col + k, n_mp)), device_id_type=MESH
        )

    order = [3 * (1 - z // 2), (2 + 3 * z) % 5, 1 + z % 2, z]
    hop_a = 2 * (1 - 2 * (z // 2))
    hop_b = 2 * (1 - 2 * (z % 2))
    hops = [hop_a, hop_b, hop_a]
    pair = z + 1 - 2 * (z % 2)

    loads = []
    for i in range(4):
        t = order[i]
        loads.append(
            pltpu.make_async_copy(
                grads.at[0, pl.ds((t * 2 + y) * shard, shard)], own.at[t], load_sem.at[i]
            )
        )
        loads[-1].start()
    state = []
    for i, (src, dst) in enumerate(((weights, w_buf), (moment1, m_buf), (moment2, v_buf))):
        state.append(pltpu.make_async_copy(src, dst, load_sem.at[4 + i]))

    other_load = pltpu.make_async_copy(
        grads.at[0, pl.ds((z * 2 + 1 - y) * shard, shard)], other, load_sem.at[7]
    )
    other_load.start()
    kept_load = pltpu.make_async_copy(average, kept, load_sem.at[8])
    kept_load.start()

    pl.semaphore_wait(barrier, n_dp - 1 + n_mp - 1)

    def not_paired(i, c, fn):
        if i == 1:
            pl.when(end)(fn)
        elif c < HALF and i == 2:
            pl.when(mid)(fn)
        else:
            fn()

    def p_copy(c):
        return pltpu.make_async_remote_copy(
            src_ref=grads.at[0, pl.ds((pair * 2 + 1 - y) * shard + c * rows, rows)],
            dst_ref=from_p.at[pl.ds(c * rows, rows)],
            send_sem=z_send,
            recv_sem=p_recv.at[c // HALF],
            device_id=(me + hop_b, col),
            device_id_type=MESH,
        )

    def y_copy(n):
        t, c = order[n // CHUNKS], n % CHUNKS
        if n // CHUNKS == 3:
            src = other.at[pl.ds(c * rows, rows)]
        else:
            src = grads.at[0, pl.ds((t * 2 + 1 - y) * shard + c * rows, rows)]
        return pltpu.make_async_remote_copy(
            src_ref=src,
            dst_ref=from_y.at[t, pl.ds(c * rows, rows)],
            send_sem=y_send,
            recv_sem=y_recv.at[n],
            device_id=(partner, col),
            device_id_type=MESH,
        )

    def z_copy(i, c):
        t = order[i]
        slot = t if i < 2 else t + (4 - t) * (z // 2)
        return pltpu.make_async_remote_copy(
            src_ref=own.at[t, pl.ds(c * rows, rows)],
            dst_ref=from_z.at[slot, pl.ds(c * rows, rows)],
            send_sem=z_send,
            recv_sem=z_recv.at[slot * CHUNKS + c],
            device_id=(me + hops[i], col),
            device_id_type=MESH,
        )

    def z_wait(slot, c):
        pltpu.make_async_remote_copy(
            src_ref=own.at[0, pl.ds(c * rows, rows)],
            dst_ref=from_z.at[slot, pl.ds(c * rows, rows)],
            send_sem=z_send,
            recv_sem=z_recv.at[slot * CHUNKS + c],
            device_id=(partner, col),
            device_id_type=MESH,
        ).wait_recv()

    def f32(ref, at, start):
        return ref[at, pl.ds(start, TILE), :].astype(jnp.float32)

    slots = 2
    far = (3 - z) * 2
    local = kept.shape[0]

    def pack():
        for dst in range(n_dp):
            first, second, count = jnp.int32(0), jnp.int32(0), jnp.int32(0)
            for k in range(local):
                hit = (owners[me * local + k] == dst).astype(jnp.int32)
                first += hit * (count == 0).astype(jnp.int32) * k
                second += hit * (count == 1).astype(jnp.int32) * k
                count += hit
            packed[dst * slots] = kept[first]
            packed[dst * slots + 1] = kept[second]

    def a_send_copy(src_ref, src, dst):
        return pltpu.make_async_remote_copy(
            src_ref=src_ref,
            dst_ref=unpacked.at[pl.ds(src * slots, slots)],
            send_sem=a_send,
            recv_sem=a_recv,
            device_id=(dst, col),
            device_id_type=MESH,
        )

    def a_copy(dst):
        return a_send_copy(packed.at[pl.ds(dst * slots, slots)], me, dst)

    def r_copy(k):
        dst = 6 * k + 1 - y
        return pltpu.make_async_remote_copy(
            src_ref=packed.at[pl.ds(dst * slots, slots)],
            dst_ref=relay.at[pl.ds(k * slots, slots)],
            send_sem=a_send,
            recv_sem=r_recv.at[k],
            device_id=(partner, col),
            device_id_type=MESH,
        )

    def f_copy(k):
        return a_send_copy(relay.at[pl.ds(k * slots, slots)], partner, 6 * k + y)

    def whole(ref, count, send_sem, recv_sem):
        part = ref.at[pl.ds(0, count)]
        return pltpu.make_async_remote_copy(
            src_ref=part,
            dst_ref=part,
            send_sem=send_sem,
            recv_sem=recv_sem,
            device_id=(partner, col),
            device_id_type=MESH,
        )

    def x_copy():
        return pltpu.make_async_remote_copy(
            src_ref=packed.at[pl.ds((far + 1 - y) * slots, slots)],
            dst_ref=relay.at[pl.ds(2 * slots, slots)],
            send_sem=a_send,
            recv_sem=r_recv.at[2],
            device_id=((2 - z // 3) * 2 + 1 - y, col),
            device_id_type=MESH,
        )

    def x_pass():
        src = (3 - pair) * 2 + 1 - y
        return a_send_copy(relay.at[pl.ds(2 * slots, slots)], src, pair * 2 + y)

    early = [y, 6 + y, far + y]
    late = [2, 3, 4, 5]

    total_chunks = 4 * CHUNKS
    def y_start(n):
        if n < total_chunks:
            not_paired(n // CHUNKS, n % CHUNKS, lambda: y_copy(n).start())

    for n in range(WINDOW):
        y_start(n)
    for c in range(HALF):
        p_copy(c).start()
    kept_load.wait()
    pack()

    @pl.when(mid)
    def _():
        for c in range(HALF, CHUNKS):
            p_copy(c).start()
        for k in range(2):
            r_copy(k).start()

    for s in state:
        s.start()

    for n in range(3 * CHUNKS):
        i, c = n // CHUNKS, n % CHUNKS
        t = order[i]
        if c == 0:
            loads[i].wait()
        if n == DIRECT_AT:

            @pl.when(mid)
            def _():
                for dst in early:
                    a_copy(dst).start()

        if n == RELAY_AT:

            @pl.when(mid)
            def _():
                for k in range(2):
                    r_copy(k).wait_recv()
                    f_copy(k).start()

        if n == PAIR_AT:
            other_load.wait()
        k = n - PAIR_AT
        if 0 <= k < CHUNKS:

            def join():
                if k % HALF == 0:
                    whole(from_p, HALF * rows, z_send, p_recv.at[k // HALF]).wait_recv()

                @pl.loop(0, rows // TILE)
                def _(b):
                    part = pl.ds(pl.multiple_of(k * rows + b * TILE, TILE), TILE)
                    val = other[part, :].astype(jnp.float32) + from_p[part, :].astype(jnp.float32)
                    other[part, :] = val.astype(jnp.bfloat16)

            if k < HALF:
                join()
            else:
                pl.when(end)(join)

        not_paired(i, c, lambda: y_copy(n).wait_recv())
        y_start(n + WINDOW)

        def add(with_y, with_z):
            if with_z:
                z_wait(t, c)

            @pl.loop(0, rows // TILE)
            def _(b):
                at = pl.multiple_of(c * rows + b * TILE, TILE)
                val = f32(own, t, at)
                if with_y:
                    val = val + f32(from_y, t, at)
                if with_z:
                    val = val + f32(from_z, t, at)
                own[t, pl.ds(at, TILE), :] = val.astype(jnp.bfloat16)

        paired_mid = i == 1
        paired_end = c < HALF and i == 2
        pl.when(mid)(functools.partial(add, not paired_mid, True))
        if not paired_end:
            pl.when(end)(functools.partial(add, True, False))
        z_copy(i, c).start()

    loads[3].wait()
    part_dp[me] = jnp.zeros((8, width // 2), jnp.float32)
    for c in range(CHUNKS):
        n = 3 * CHUNKS + c
        y_copy(n).wait_recv()
        y_start(n + WINDOW)
        z_wait(z, c)

        def keep(at, val):
            summed[pl.ds(at, TILE), :] = val
            squares = jnp.sum((val * val).reshape(TILE // 8, 8, width), axis=0)
            part_dp[me] += squares[:, : width // 2] + squares[:, width // 2 :]

        @pl.when(mid)
        def _():
            z_wait(4, c)

            @pl.loop(0, rows // TILE)
            def _(b):
                at = pl.multiple_of(c * rows + b * TILE, TILE)
                keep(at, f32(own, z, at) + f32(from_y, z, at) + f32(from_z, z, at) + f32(from_z, 4, at))

        @pl.when(end)
        def _():
            @pl.loop(0, rows // TILE)
            def _(b):
                at = pl.multiple_of(c * rows + b * TILE, TILE)
                keep(at, f32(own, z, at) + f32(from_y, z, at) + f32(from_z, z, at))

    def dp_copy(k):
        return pltpu.make_async_remote_copy(
            src_ref=part_dp.at[me],
            dst_ref=part_dp.at[me],
            send_sem=dp_send,
            recv_sem=dp_recv,
            device_id=(lax.rem(me + k, n_dp), col),
            device_id_type=MESH,
        )

    def mp_copy(k):
        return pltpu.make_async_remote_copy(
            src_ref=part_mp.at[col],
            dst_ref=part_mp.at[col],
            send_sem=mp_send,
            recv_sem=mp_recv,
            device_id=(me, lax.rem(col + k, n_mp)),
            device_id_type=MESH,
        )

    all_dp = whole(part_dp, n_dp - 1, dp_send, dp_recv)
    all_mp = whole(part_mp, n_mp - 1, mp_send, mp_recv)

    for k in range(1, n_dp):
        dp_copy(k).start()
    a_own = pltpu.make_async_copy(
        packed.at[pl.ds(me * slots, slots)], unpacked.at[pl.ds(me * slots, slots)], a_local
    )
    a_own.start()
    all_dp.wait_recv()
    group = part_dp[0]
    for k in range(1, n_dp):
        group = group + part_dp[k]
    part_mp[col] = group
    for k in range(1, n_mp):
        mp_copy(k).start()
    a_copy(partner).start()

    @pl.when(end)
    def _():
        a_copy(far + y).start()
        x_copy().start()

    @pl.when(mid)
    def _():
        a_copy(far + 1 - y).start()

    for s in state:
        s.wait()
    all_mp.wait_recv()
    everything = part_mp[0]
    for k in range(1, n_mp):
        everything = everything + part_mp[k]
    total = jnp.sum(everything, axis=(0, 1), keepdims=True)
    factor = jnp.minimum(1.0, limit / (jnp.sqrt(total) + 1e-06))

    def g_copy(src_ref, dev, c, send_sem, recv_sem, target):
        return pltpu.make_async_remote_copy(
            src_ref=src_ref,
            dst_ref=gathered.at[pl.ds(dev * shard + c * rows, rows)],
            send_sem=send_sem,
            recv_sem=recv_sem,
            device_id=(target, col),
            device_id_type=MESH,
        )

    def held(dev, c):
        return gathered.at[pl.ds(dev * shard + c * rows, rows)]

    def step_sem(plane, c):
        return y_recv.at[plane * CHUNKS + c]

    def own_y(c):
        return g_copy(new_buf.at[pl.ds(c * rows, rows)], me, c, gy_send, step_sem(z, c), partner)

    def own_z(c, hop):
        return g_copy(new_buf.at[pl.ds(c * rows, rows)], me, c, gz_send, step_sem(z, c), me + hop)

    def fwd_y(i, c):
        dev = order[i] * 2 + y
        return g_copy(held(dev, c), dev, c, gy_send, g_rest, partner)

    def fwd_z(i, c):
        dev = order[i] * 2 + y
        return g_copy(held(dev, c), dev, c, gz_send, step_sem(order[i], c), me - hops[i])

    def fwd_p(c):
        dev = z * 2 + 1 - y
        return g_copy(held(dev, c), dev, c, gz_send, g_rest, me + hop_b)

    def g_wait(plane, side, c):
        g_copy(
            new_buf.at[pl.ds(c * rows, rows)], plane * 2 + side, c, gy_send, step_sem(plane, c), partner
        ).wait_recv()

    def local_copies(c):
        part = pl.ds(c * rows, rows)
        return [
            pltpu.make_async_copy(
                new_buf.at[part], gathered.at[pl.ds(me * shard + c * rows, rows)], g_local
            ),
            pltpu.make_async_copy(m_buf.at[part], out_m.at[part], o_sem.at[0]),
            pltpu.make_async_copy(v_buf.at[part], out_v.at[part], o_sem.at[1]),
        ]

    for c in range(CHUNKS):

        @pl.loop(0, rows // TILE)
        def _(b):
            at = pl.multiple_of(c * rows + b * TILE, TILE)
            matrix_id = (me * shard + at) // BLOCK
            decayed = jnp.where((matrix_id != 4) & (matrix_id < nmat - EMAT), 1.0, 0.0)
            part = pl.ds(at, TILE)
            new_w, new_m, new_v = update(
                summed[part, :] * factor, w_buf[part, :], m_buf[part, :], v_buf[part, :], decayed
            )
            m_buf[part, :] = new_m
            v_buf[part, :] = new_v
            new_buf[part, :] = new_w.astype(jnp.bfloat16)

        own_y(c).start()

        @pl.when(z < 3)
        def _():
            own_z(c, 2).start()

        @pl.when(z > 0)
        def _():
            own_z(c, -2).start()

        for copy in local_copies(c):
            copy.start()

    @pl.when(end)
    def _():
        for dst in late:
            a_copy(dst).start()

    def fwd_q(c):
        dev = z * 2 + 1 - y
        return g_copy(held(dev, c), dev, c, gz_send, g_rest, me - hop_b)

    def passes_y(i, c, fn):
        at_end = i != 2 or c >= SPLIT
        at_mid = i != 1 and not (i == 2 and c in CROSS)
        if at_end and at_mid:
            fn()
        elif at_end:
            pl.when(end)(fn)
        elif at_mid:
            pl.when(mid)(fn)

    def pass_on(c, at_end):
        g_wait(z, 1 - y, c)
        if at_end or c < SPLIT:
            fwd_p(c).start()
        if not at_end and c in CROSS:
            fwd_q(c).start()

    for i in (2, 1, 0):
        for c in range(CHUNKS):
            g_wait(order[i], y, c)

            @pl.when(mid)
            def _():
                fwd_z(i, c).start()

            passes_y(i, c, lambda: fwd_y(i, c).start())
            if i == 2:
                pl.when(end)(lambda: pass_on(c, True))
                if c < SPLIT - KEEP or c in CROSS:
                    pl.when(mid)(lambda: pass_on(c, False))
                if c == PASS_AT:

                    @pl.when(mid)
                    def _():
                        whole(relay, slots, a_send, r_recv.at[2]).wait_recv()
                        x_pass().start()

    @pl.when(mid)
    def _():
        for c in range(CHUNKS):
            if not (c < SPLIT - KEEP or c in CROSS):
                pass_on(c, False)

    def drain(ref, count, sem):
        whole(ref, count, sem, g_rest).wait_send()

    @pl.when(end)
    def _():
        drain(gathered, (4 * CHUNKS - HALF) * rows, y_send)
        drain(gathered, (3 * CHUNKS + HALF) * rows, z_send)
        drain(gathered, (4 * CHUNKS - SPLIT) * rows, gy_send)
        drain(gathered, 2 * CHUNKS * rows, gz_send)
        drain(unpacked, 7 * slots, a_send)

    @pl.when(mid)
    def _():
        drain(gathered, 3 * CHUNKS * rows, y_send)
        drain(gathered, 4 * CHUNKS * rows, z_send)
        drain(gathered, (3 * CHUNKS - len(CROSS)) * rows, gy_send)
        drain(gathered, (5 * CHUNKS + SPLIT + len(CROSS)) * rows, gz_send)
        drain(gathered, 10 * slots * BLOCK, a_send)

    all_dp.wait_send()
    all_mp.wait_send()
    a_own.wait()
    pltpu.make_async_copy(new_buf, gathered.at[pl.ds(me * shard, shard)], g_local).wait()
    pltpu.make_async_copy(m_buf, out_m, o_sem.at[0]).wait()
    pltpu.make_async_copy(v_buf, out_v, o_sem.at[1]).wait()
    whole(unpacked, (n_dp - 1) * slots, a_send, a_recv).wait_recv()
    whole(gathered, 3 * CHUNKS * rows, gz_send, g_rest).wait_recv()


def finish_kernel(
    n_dp, most, nmat, owners, gathered, unpacked, m_in, v_in,
    out_w, owned, m_out, v_out, w_buf, fresh_buf, matrix_at, slot_at, w_sem, fresh_sem, state_sem
):
    me = lax.axis_index("dp")
    local = nmat // n_dp
    parts = gathered.shape[0] // PART

    state = [
        pltpu.make_async_copy(m_in, m_out, state_sem.at[0]),
        pltpu.make_async_copy(v_in, v_out, state_sem.at[1]),
    ]

    def w_copy(i):
        return pltpu.make_async_copy(
            w_buf.at[i % DEPTH], out_w.at[pl.ds(i * PART, PART)], w_sem.at[i % DEPTH]
        )

    def fresh_copy(j):
        return pltpu.make_async_copy(
            fresh_buf.at[j], owned.at[0, pl.ds(j * BLOCK, BLOCK)], fresh_sem.at[j]
        )

    def widen(i):
        if i >= DEPTH:
            w_copy(i - DEPTH).wait()

        @pl.loop(0, PART // TILE)
        def _(b):
            at = pl.multiple_of(b * TILE, TILE)
            w_buf[i % DEPTH, pl.ds(at, TILE), :] = gathered[pl.ds(i * PART + at, TILE), :].astype(
                jnp.float32
            )

        w_copy(i).start()

    def scan(src, kept):
        def one(k, carry):
            kept, here = carry
            g = src * local + k
            mine = (owners[g] == me).astype(jnp.int32)
            matrix_at[kept] = g
            slot_at[kept] = src * 2 + here
            return kept + mine, here + mine

        return lax.fori_loop(0, local, one, (kept, jnp.int32(0)))[0]

    def pick(j, count):
        @pl.when(j < count)
        def _():
            w_part = pl.ds(pl.multiple_of(matrix_at[j] * BLOCK, BLOCK), BLOCK)
            fresh = average_decay * unpacked[slot_at[j]].astype(jnp.float32) + (
                1.0 - average_decay
            ) * gathered[w_part, :].astype(jnp.float32)
            fresh_buf[j] = fresh.astype(jnp.bfloat16)

        @pl.when(j >= count)
        def _():
            fresh_buf[j] = jnp.zeros(fresh_buf.shape[1:], jnp.bfloat16)

        fresh_copy(j).start()

    for i in range(DEPTH):
        widen(i)
    for copy in state:
        copy.start()
    count = lax.fori_loop(0, n_dp, scan, jnp.int32(0))
    for j in range(most):
        pick(j, count)
    for i in range(DEPTH, parts):
        widen(i)
    for i in range(parts - DEPTH, parts):
        w_copy(i).wait()
    for j in range(most):
        fresh_copy(j).wait()
    for copy in state:
        copy.wait()


def grid_shards(n_dp, n_mp, limit, grads, weights, moment1, moment2, average, owners):
    shard, width = weights.shape
    local = shard // BLOCK
    most = local + local // 2
    nmat = owners.shape[0]
    total_rows = grads.shape[1]
    owner_col = pltpu.with_memory_space_constraint(owners[:, 0], pltpu.HBM)
    any_spec = pl.BlockSpec(memory_space=pl.ANY)
    smem_spec = pl.BlockSpec(memory_space=pltpu.SMEM)
    bf16, f32 = jnp.bfloat16, jnp.float32
    dma = pltpu.SemaphoreType.DMA

    average = average.reshape(local, BLOCK, width)
    grads, weights, moment1, moment2, average = (
        pltpu.with_memory_space_constraint(a, pltpu.HBM)
        for a in (grads, weights, moment1, moment2, average)
    )
    gathered, new_m, new_v, unpacked = pl.pallas_call(
        functools.partial(step_kernel, n_dp, n_mp, limit, nmat),
        out_shape=(
            pltpu.VMEM((total_rows, width), bf16),
            pltpu.VMEM((shard, width), f32),
            pltpu.VMEM((shard, width), f32),
            pltpu.VMEM((n_dp * 2, BLOCK, width), bf16),
        ),
        in_specs=[smem_spec] + [any_spec] * 5,
        out_specs=(any_spec,) * 4,
        scratch_shapes=[
            pltpu.VMEM((4, shard, width), bf16),
            pltpu.VMEM((4, shard, width), bf16),
            pltpu.VMEM((5, shard, width), bf16),
            pltpu.VMEM((shard, width), f32),
            pltpu.VMEM((shard, width), f32),
            pltpu.VMEM((shard, width), f32),
            pltpu.VMEM((shard, width), f32),
            pltpu.VMEM((shard, width), bf16),
            pltpu.VMEM((n_dp, 8, width // 2), f32),
            pltpu.VMEM((n_mp, 8, width // 2), f32),
            pltpu.VMEM((shard, width), bf16),
            pltpu.VMEM((shard, width), bf16),
            pltpu.VMEM((local, BLOCK, width), bf16),
            pltpu.VMEM((n_dp * 2, BLOCK, width), bf16),
            pltpu.VMEM((6, BLOCK, width), bf16),
            dma((9,)),
            dma,
            dma((4 * CHUNKS,)),
            dma,
            dma((5 * CHUNKS,)),
            dma,
            dma,
            dma,
            dma,
            dma,
            dma,
            dma,
            dma((3,)),
            dma,
            dma,
            dma,
            dma,
            dma((2,)),
            dma((2,)),
        ],
        compiler_params=pltpu.CompilerParams(
            collective_id=0, has_side_effects=True, vmem_limit_bytes=32 * 2**20
        ),
    )(owner_col, grads, weights, moment1, moment2, average)

    gathered, new_m, new_v, unpacked = (
        pltpu.with_memory_space_constraint(a, pltpu.VMEM) for a in (gathered, new_m, new_v, unpacked)
    )
    vmem_spec = pl.BlockSpec(memory_space=pltpu.VMEM)
    new_full, owned, new_m, new_v = pl.pallas_call(
        functools.partial(finish_kernel, n_dp, most, nmat),
        out_shape=(
            jax.ShapeDtypeStruct((total_rows, width), f32),
            jax.ShapeDtypeStruct((1, most * BLOCK, width), bf16),
            jax.ShapeDtypeStruct((shard, width), f32),
            jax.ShapeDtypeStruct((shard, width), f32),
        ),
        in_specs=[smem_spec, vmem_spec, vmem_spec, any_spec, any_spec],
        out_specs=(any_spec,) * 4,
        scratch_shapes=[
            pltpu.VMEM((DEPTH, PART, width), f32),
            pltpu.VMEM((most, BLOCK, width), bf16),
            pltpu.SMEM((most + 1,), jnp.int32),
            pltpu.SMEM((most + 1,), jnp.int32),
            dma((DEPTH,)),
            dma((most,)),
            dma((2,)),
        ],
        compiler_params=pltpu.CompilerParams(vmem_limit_bytes=16 * 2**20),
    )(owner_col, gathered, unpacked, new_m, new_v)
    return (new_full, new_m, new_v, owned)


def solution(mesh):
    n_dp, n_mp = mesh.shape["dp"], mesh.shape["mp"]

    def step(grads, weights, moment1, moment2, average, owners):
        limit = float(weights.shape[0] * weights.shape[1]) ** 0.5
        if n_dp == 8:
            body = functools.partial(grid_shards, n_dp, n_mp, limit)
        else:
            body = functools.partial(plain_shards, limit)
        placed = (P("dp", None, "mp"), P("dp", "mp"), P("dp", "mp"), P("dp", "mp"), P("dp", "mp"), P())
        return jax.shard_map(
            body,
            mesh=mesh,
            in_specs=placed,
            out_specs=(P(None, "mp"), P("dp", "mp"), P("dp", "mp"), P("dp", None, "mp")),
            check_vma=False,
        )(grads, weights, moment1, moment2, average, owners)

    return step
```

```python
import functools

import jax
import jax.numpy as jnp
from jax import lax
from jax.experimental import pallas as pl
from jax.experimental.pallas import tpu as pltpu
from jax.sharding import PartitionSpec as P

BLOCK = 256
EMAT = 32
MESH = pl.DeviceIdType.MESH


learning = 0.05
beta_one = 0.9
beta_two = 0.95
epsilon = 1e-08
weight_decay = 0.1
average_decay = 0.9
step_count = 10


def update(clipped, weights, moment1, moment2, decayed):
    new_m = beta_one * moment1 + (1.0 - beta_one) * clipped
    new_v = beta_two * moment2 + (1.0 - beta_two) * clipped * clipped
    v_hat = new_v * (1.0 / (1.0 - beta_two**step_count))
    rate = learning / (1.0 - beta_one**step_count)
    new_w = weights * (1.0 - learning * weight_decay * decayed) - rate * new_m / (
        jnp.sqrt(v_hat) + epsilon
    )
    return (new_w, new_m, new_v)


def pick_owned(fresh_full, owner_col, owner_id, most, nmat):
    flags = owner_col == owner_id
    ids = jnp.arange(nmat, dtype=jnp.int32)
    position = jnp.sum((flags[None, :] & (ids[None, :] <= ids[:, None])).astype(jnp.int32), axis=1) - 1
    slots = jnp.arange(most, dtype=jnp.int32)
    select = (flags[None, :] & (position[None, :] == slots[:, None])).astype(jnp.bfloat16)
    stacked = fresh_full.reshape(nmat, -1)
    picked = jnp.dot(select, stacked, preferred_element_type=jnp.float32)
    return picked.astype(jnp.bfloat16).reshape(1, most * BLOCK, -1)


def plain_shards(limit, grads, weights, moment1, moment2, average, owners):
    shard_rows = weights.shape[0]
    local_count = shard_rows // BLOCK
    most = local_count + local_count // 2
    nmat = owners.shape[0]
    my_index = lax.axis_index("dp")
    summed = lax.psum_scatter(grads[0], "dp", scatter_dimension=0, tiled=True).astype(jnp.float32)
    total = lax.psum(jnp.sum(summed * summed), ("dp", "mp"))
    factor = jnp.minimum(1.0, limit / (jnp.sqrt(total) + 1e-06))
    row_ids = my_index * shard_rows + jnp.arange(shard_rows, dtype=jnp.int32)
    matrix_id = row_ids // BLOCK
    decayed = ((matrix_id != 4) & (matrix_id < nmat - EMAT)).astype(jnp.float32)[:, None]
    new_w, new_m, new_v = update(summed * factor, weights, moment1, moment2, decayed)
    new_full = lax.all_gather(new_w, "dp", axis=0, tiled=True)
    fresh = (average_decay * average.astype(jnp.float32) + (1.0 - average_decay) * new_w).astype(
        jnp.bfloat16
    )
    fresh_full = lax.all_gather(fresh, "dp", axis=0, tiled=True)
    owned = pick_owned(fresh_full, owners[:, 0], my_index, most, nmat)
    return (new_full, new_m, new_v, owned)


CHUNKS = 8
HALF = CHUNKS // 2
PART = 512
DEPTH = 8
DIRECT_AT = 2
RELAY_AT = 12
PAIR_AT = 10
KEEP = 2
SPLIT = 3
CROSS = (0, 4)
PASS_AT = 2
WINDOW = 10
TILE = 64


def step_kernel(
    n_dp, n_mp, limit, nmat,
    owners, grads, weights, moment1, moment2, average,
    gathered, out_m, out_v, unpacked,
    own, from_y, from_z, summed, w_buf, m_buf, v_buf, new_buf, part_dp, part_mp, other, from_p,
    kept, packed, relay,
    load_sem, y_send, y_recv, z_send, z_recv, dp_send, dp_recv, mp_send, mp_recv,
    a_send, a_recv, a_local, r_recv, gy_send, gz_send, g_rest, g_local, o_sem, p_recv,
):
    me = lax.axis_index("dp")
    col = lax.axis_index("mp")
    z, y = me // 2, me % 2
    partner = me + 1 - 2 * y
    shard = weights.shape[0]
    rows = shard // CHUNKS
    width = weights.shape[1]
    mid = (z == 1) | (z == 2)
    end = (z == 0) | (z == 3)

    barrier = pltpu.get_barrier_semaphore()
    for k in range(1, n_dp):
        pl.semaphore_signal(
            barrier, inc=1, device_id=(lax.rem(me + k, n_dp), col), device_id_type=MESH
        )
    for k in range(1, n_mp):
        pl.semaphore_signal(
            barrier, inc=1, device_id=(me, lax.rem(col + k, n_mp)), device_id_type=MESH
        )

    order = [3 * (1 - z // 2), (2 + 3 * z) % 5, 1 + z % 2, z]
    hop_a = 2 * (1 - 2 * (z // 2))
    hop_b = 2 * (1 - 2 * (z % 2))
    hops = [hop_a, hop_b, hop_a]
    pair = z + 1 - 2 * (z % 2)

    loads = []
    for i in range(4):
        t = order[i]
        loads.append(
            pltpu.make_async_copy(
                grads.at[0, pl.ds((t * 2 + y) * shard, shard)], own.at[t], load_sem.at[i]
            )
        )
        loads[-1].start()
    state = []
    for i, (src, dst) in enumerate(((weights, w_buf), (moment1, m_buf), (moment2, v_buf))):
        state.append(pltpu.make_async_copy(src, dst, load_sem.at[4 + i]))

    other_load = pltpu.make_async_copy(
        grads.at[0, pl.ds((z * 2 + 1 - y) * shard, shard)], other, load_sem.at[7]
    )
    other_load.start()
    kept_load = pltpu.make_async_copy(average, kept, load_sem.at[8])
    kept_load.start()

    pl.semaphore_wait(barrier, n_dp - 1 + n_mp - 1)

    def not_paired(i, c, fn):
        if i == 1:
            pl.when(end)(fn)
        elif c < HALF and i == 2:
            pl.when(mid)(fn)
        else:
            fn()

    def p_copy(c):
        return pltpu.make_async_remote_copy(
            src_ref=grads.at[0, pl.ds((pair * 2 + 1 - y) * shard + c * rows, rows)],
            dst_ref=from_p.at[pl.ds(c * rows, rows)],
            send_sem=z_send,
            recv_sem=p_recv.at[c // HALF],
            device_id=(me + hop_b, col),
            device_id_type=MESH,
        )

    def y_copy(n):
        t, c = order[n // CHUNKS], n % CHUNKS
        if n // CHUNKS == 3:
            src = other.at[pl.ds(c * rows, rows)]
        else:
            src = grads.at[0, pl.ds((t * 2 + 1 - y) * shard + c * rows, rows)]
        return pltpu.make_async_remote_copy(
            src_ref=src,
            dst_ref=from_y.at[t, pl.ds(c * rows, rows)],
            send_sem=y_send,
            recv_sem=y_recv.at[n],
            device_id=(partner, col),
            device_id_type=MESH,
        )

    def z_copy(i, c):
        t = order[i]
        slot = t if i < 2 else t + (4 - t) * (z // 2)
        return pltpu.make_async_remote_copy(
            src_ref=own.at[t, pl.ds(c * rows, rows)],
            dst_ref=from_z.at[slot, pl.ds(c * rows, rows)],
            send_sem=z_send,
            recv_sem=z_recv.at[slot * CHUNKS + c],
            device_id=(me + hops[i], col),
            device_id_type=MESH,
        )

    def z_wait(slot, c):
        pltpu.make_async_remote_copy(
            src_ref=own.at[0, pl.ds(c * rows, rows)],
            dst_ref=from_z.at[slot, pl.ds(c * rows, rows)],
            send_sem=z_send,
            recv_sem=z_recv.at[slot * CHUNKS + c],
            device_id=(partner, col),
            device_id_type=MESH,
        ).wait_recv()

    def f32(ref, at, start):
        return ref[at, pl.ds(start, TILE), :].astype(jnp.float32)

    slots = 2
    far = (3 - z) * 2
    local = kept.shape[0]

    def pack():
        for dst in range(n_dp):
            first, second, count = jnp.int32(0), jnp.int32(0), jnp.int32(0)
            for k in range(local):
                hit = (owners[me * local + k] == dst).astype(jnp.int32)
                first += hit * (count == 0).astype(jnp.int32) * k
                second += hit * (count == 1).astype(jnp.int32) * k
                count += hit
            packed[dst * slots] = kept[first]
            packed[dst * slots + 1] = kept[second]

    def a_send_copy(src_ref, src, dst):
        return pltpu.make_async_remote_copy(
            src_ref=src_ref,
            dst_ref=unpacked.at[pl.ds(src * slots, slots)],
            send_sem=a_send,
            recv_sem=a_recv,
            device_id=(dst, col),
            device_id_type=MESH,
        )

    def a_copy(dst):
        return a_send_copy(packed.at[pl.ds(dst * slots, slots)], me, dst)

    def r_copy(k):
        dst = 6 * k + 1 - y
        return pltpu.make_async_remote_copy(
            src_ref=packed.at[pl.ds(dst * slots, slots)],
            dst_ref=relay.at[pl.ds(k * slots, slots)],
            send_sem=a_send,
            recv_sem=r_recv.at[k],
            device_id=(partner, col),
            device_id_type=MESH,
        )

    def f_copy(k):
        return a_send_copy(relay.at[pl.ds(k * slots, slots)], partner, 6 * k + y)

    def whole(ref, count, send_sem, recv_sem):
        part = ref.at[pl.ds(0, count)]
        return pltpu.make_async_remote_copy(
            src_ref=part,
            dst_ref=part,
            send_sem=send_sem,
            recv_sem=recv_sem,
            device_id=(partner, col),
            device_id_type=MESH,
        )

    def x_copy():
        return pltpu.make_async_remote_copy(
            src_ref=packed.at[pl.ds((far + 1 - y) * slots, slots)],
            dst_ref=relay.at[pl.ds(2 * slots, slots)],
            send_sem=a_send,
            recv_sem=r_recv.at[2],
            device_id=((2 - z // 3) * 2 + 1 - y, col),
            device_id_type=MESH,
        )

    def x_pass():
        src = (3 - pair) * 2 + 1 - y
        return a_send_copy(relay.at[pl.ds(2 * slots, slots)], src, pair * 2 + y)

    early = [y, 6 + y, far + y]
    late = [2, 3, 4, 5]

    total_chunks = 4 * CHUNKS
    def y_start(n):
        if n < total_chunks:
            not_paired(n // CHUNKS, n % CHUNKS, lambda: y_copy(n).start())

    for n in range(WINDOW):
        y_start(n)
    for c in range(HALF):
        p_copy(c).start()
    kept_load.wait()
    pack()

    @pl.when(mid)
    def _():
        for c in range(HALF, CHUNKS):
            p_copy(c).start()
        for k in range(2):
            r_copy(k).start()

    for s in state:
        s.start()

    for n in range(3 * CHUNKS):
        i, c = n // CHUNKS, n % CHUNKS
        t = order[i]
        if c == 0:
            loads[i].wait()
        if n == DIRECT_AT:

            @pl.when(mid)
            def _():
                for dst in early:
                    a_copy(dst).start()

        if n == RELAY_AT:

            @pl.when(mid)
            def _():
                for k in range(2):
                    r_copy(k).wait_recv()
                    f_copy(k).start()

        if n == PAIR_AT:
            other_load.wait()
        k = n - PAIR_AT
        if 0 <= k < CHUNKS:

            def join():
                if k % HALF == 0:
                    whole(from_p, HALF * rows, z_send, p_recv.at[k // HALF]).wait_recv()

                @pl.loop(0, rows // TILE)
                def _(b):
                    part = pl.ds(pl.multiple_of(k * rows + b * TILE, TILE), TILE)
                    val = other[part, :].astype(jnp.float32) + from_p[part, :].astype(jnp.float32)
                    other[part, :] = val.astype(jnp.bfloat16)

            if k < HALF:
                join()
            else:
                pl.when(end)(join)

        not_paired(i, c, lambda: y_copy(n).wait_recv())
        y_start(n + WINDOW)

        def add(with_y, with_z):
            if with_z:
                z_wait(t, c)

            @pl.loop(0, rows // TILE)
            def _(b):
                at = pl.multiple_of(c * rows + b * TILE, TILE)
                val = f32(own, t, at)
                if with_y:
                    val = val + f32(from_y, t, at)
                if with_z:
                    val = val + f32(from_z, t, at)
                own[t, pl.ds(at, TILE), :] = val.astype(jnp.bfloat16)

        paired_mid = i == 1
        paired_end = c < HALF and i == 2
        pl.when(mid)(functools.partial(add, not paired_mid, True))
        if not paired_end:
            pl.when(end)(functools.partial(add, True, False))
        z_copy(i, c).start()

    loads[3].wait()
    part_dp[me] = jnp.zeros((8, width // 2), jnp.float32)
    for c in range(CHUNKS):
        n = 3 * CHUNKS + c
        y_copy(n).wait_recv()
        y_start(n + WINDOW)
        z_wait(z, c)

        def keep(at, val):
            summed[pl.ds(at, TILE), :] = val
            squares = jnp.sum((val * val).reshape(TILE // 8, 8, width), axis=0)
            part_dp[me] += squares[:, : width // 2] + squares[:, width // 2 :]

        @pl.when(mid)
        def _():
            z_wait(4, c)

            @pl.loop(0, rows // TILE)
            def _(b):
                at = pl.multiple_of(c * rows + b * TILE, TILE)
                keep(at, f32(own, z, at) + f32(from_y, z, at) + f32(from_z, z, at) + f32(from_z, 4, at))

        @pl.when(end)
        def _():
            @pl.loop(0, rows // TILE)
            def _(b):
                at = pl.multiple_of(c * rows + b * TILE, TILE)
                keep(at, f32(own, z, at) + f32(from_y, z, at) + f32(from_z, z, at))

    def dp_copy(k):
        return pltpu.make_async_remote_copy(
            src_ref=part_dp.at[me],
            dst_ref=part_dp.at[me],
            send_sem=dp_send,
            recv_sem=dp_recv,
            device_id=(lax.rem(me + k, n_dp), col),
            device_id_type=MESH,
        )

    def mp_copy(k):
        return pltpu.make_async_remote_copy(
            src_ref=part_mp.at[col],
            dst_ref=part_mp.at[col],
            send_sem=mp_send,
            recv_sem=mp_recv,
            device_id=(me, lax.rem(col + k, n_mp)),
            device_id_type=MESH,
        )

    all_dp = whole(part_dp, n_dp - 1, dp_send, dp_recv)
    all_mp = whole(part_mp, n_mp - 1, mp_send, mp_recv)

    for k in range(1, n_dp):
        dp_copy(k).start()
    a_own = pltpu.make_async_copy(
        packed.at[pl.ds(me * slots, slots)], unpacked.at[pl.ds(me * slots, slots)], a_local
    )
    a_own.start()
    all_dp.wait_recv()
    group = part_dp[0]
    for k in range(1, n_dp):
        group = group + part_dp[k]
    part_mp[col] = group
    for k in range(1, n_mp):
        mp_copy(k).start()
    a_copy(partner).start()

    @pl.when(end)
    def _():
        a_copy(far + y).start()
        x_copy().start()

    @pl.when(mid)
    def _():
        a_copy(far + 1 - y).start()

    for s in state:
        s.wait()
    all_mp.wait_recv()
    everything = part_mp[0]
    for k in range(1, n_mp):
        everything = everything + part_mp[k]
    total = jnp.sum(everything, axis=(0, 1), keepdims=True)
    factor = jnp.minimum(1.0, limit / (jnp.sqrt(total) + 1e-06))

    def g_copy(src_ref, dev, c, send_sem, recv_sem, target):
        return pltpu.make_async_remote_copy(
            src_ref=src_ref,
            dst_ref=gathered.at[pl.ds(dev * shard + c * rows, rows)],
            send_sem=send_sem,
            recv_sem=recv_sem,
            device_id=(target, col),
            device_id_type=MESH,
        )

    def held(dev, c):
        return gathered.at[pl.ds(dev * shard + c * rows, rows)]

    def step_sem(plane, c):
        return y_recv.at[plane * CHUNKS + c]

    def own_y(c):
        return g_copy(new_buf.at[pl.ds(c * rows, rows)], me, c, gy_send, step_sem(z, c), partner)

    def own_z(c, hop):
        return g_copy(new_buf.at[pl.ds(c * rows, rows)], me, c, gz_send, step_sem(z, c), me + hop)

    def fwd_y(i, c):
        dev = order[i] * 2 + y
        return g_copy(held(dev, c), dev, c, gy_send, g_rest, partner)

    def fwd_z(i, c):
        dev = order[i] * 2 + y
        return g_copy(held(dev, c), dev, c, gz_send, step_sem(order[i], c), me - hops[i])

    def fwd_p(c):
        dev = z * 2 + 1 - y
        return g_copy(held(dev, c), dev, c, gz_send, g_rest, me + hop_b)

    def g_wait(plane, side, c):
        g_copy(
            new_buf.at[pl.ds(c * rows, rows)], plane * 2 + side, c, gy_send, step_sem(plane, c), partner
        ).wait_recv()

    def local_copies(c):
        part = pl.ds(c * rows, rows)
        return [
            pltpu.make_async_copy(
                new_buf.at[part], gathered.at[pl.ds(me * shard + c * rows, rows)], g_local
            ),
            pltpu.make_async_copy(m_buf.at[part], out_m.at[part], o_sem.at[0]),
            pltpu.make_async_copy(v_buf.at[part], out_v.at[part], o_sem.at[1]),
        ]

    for c in range(CHUNKS):

        @pl.loop(0, rows // TILE)
        def _(b):
            at = pl.multiple_of(c * rows + b * TILE, TILE)
            matrix_id = (me * shard + at) // BLOCK
            decayed = jnp.where((matrix_id != 4) & (matrix_id < nmat - EMAT), 1.0, 0.0)
            part = pl.ds(at, TILE)
            new_w, new_m, new_v = update(
                summed[part, :] * factor, w_buf[part, :], m_buf[part, :], v_buf[part, :], decayed
            )
            m_buf[part, :] = new_m
            v_buf[part, :] = new_v
            new_buf[part, :] = new_w.astype(jnp.bfloat16)

        own_y(c).start()

        @pl.when(z < 3)
        def _():
            own_z(c, 2).start()

        @pl.when(z > 0)
        def _():
            own_z(c, -2).start()

        for copy in local_copies(c):
            copy.start()

    @pl.when(end)
    def _():
        for dst in late:
            a_copy(dst).start()

    def fwd_q(c):
        dev = z * 2 + 1 - y
        return g_copy(held(dev, c), dev, c, gz_send, g_rest, me - hop_b)

    def passes_y(i, c, fn):
        at_end = i != 2 or c >= SPLIT
        at_mid = i != 1 and not (i == 2 and c in CROSS)
        if at_end and at_mid:
            fn()
        elif at_end:
            pl.when(end)(fn)
        elif at_mid:
            pl.when(mid)(fn)

    def pass_on(c, at_end):
        g_wait(z, 1 - y, c)
        if at_end or c < SPLIT:
            fwd_p(c).start()
        if not at_end and c in CROSS:
            fwd_q(c).start()

    for i in (2, 1, 0):
        for c in range(CHUNKS):
            g_wait(order[i], y, c)

            @pl.when(mid)
            def _():
                fwd_z(i, c).start()

            passes_y(i, c, lambda: fwd_y(i, c).start())
            if i == 2:
                pl.when(end)(lambda: pass_on(c, True))
                if c < SPLIT - KEEP or c in CROSS:
                    pl.when(mid)(lambda: pass_on(c, False))
                if c == PASS_AT:

                    @pl.when(mid)
                    def _():
                        whole(relay, slots, a_send, r_recv.at[2]).wait_recv()
                        x_pass().start()

    @pl.when(mid)
    def _():
        for c in range(CHUNKS):
            if not (c < SPLIT - KEEP or c in CROSS):
                pass_on(c, False)

    def drain(ref, count, sem):
        whole(ref, count, sem, g_rest).wait_send()

    @pl.when(end)
    def _():
        drain(gathered, (4 * CHUNKS - HALF) * rows, y_send)
        drain(gathered, (3 * CHUNKS + HALF) * rows, z_send)
        drain(gathered, (4 * CHUNKS - SPLIT) * rows, gy_send)
        drain(gathered, 2 * CHUNKS * rows, gz_send)
        drain(unpacked, 7 * slots, a_send)

    @pl.when(mid)
    def _():
        drain(gathered, 3 * CHUNKS * rows, y_send)
        drain(gathered, 4 * CHUNKS * rows, z_send)
        drain(gathered, (3 * CHUNKS - len(CROSS)) * rows, gy_send)
        drain(gathered, (5 * CHUNKS + SPLIT + len(CROSS)) * rows, gz_send)
        drain(gathered, 10 * slots * BLOCK, a_send)

    all_dp.wait_send()
    all_mp.wait_send()
    a_own.wait()
    pltpu.make_async_copy(new_buf, gathered.at[pl.ds(me * shard, shard)], g_local).wait()
    pltpu.make_async_copy(m_buf, out_m, o_sem.at[0]).wait()
    pltpu.make_async_copy(v_buf, out_v, o_sem.at[1]).wait()
    whole(unpacked, (n_dp - 1) * slots, a_send, a_recv).wait_recv()
    whole(gathered, 3 * CHUNKS * rows, gz_send, g_rest).wait_recv()


def finish_kernel(
    n_dp, most, nmat, owners, gathered, unpacked, m_in, v_in,
    out_w, owned, m_out, v_out, w_buf, fresh_buf, matrix_at, slot_at, w_sem, fresh_sem, state_sem
):
    me = lax.axis_index("dp")
    local = nmat // n_dp
    parts = gathered.shape[0] // PART

    state = [
        pltpu.make_async_copy(m_in, m_out, state_sem.at[0]),
        pltpu.make_async_copy(v_in, v_out, state_sem.at[1]),
    ]

    def w_copy(i):
        return pltpu.make_async_copy(
            w_buf.at[i % DEPTH], out_w.at[pl.ds(i * PART, PART)], w_sem.at[i % DEPTH]
        )

    def fresh_copy(j):
        return pltpu.make_async_copy(
            fresh_buf.at[j], owned.at[0, pl.ds(j * BLOCK, BLOCK)], fresh_sem.at[j]
        )

    def widen(i):
        if i >= DEPTH:
            w_copy(i - DEPTH).wait()

        @pl.loop(0, PART // TILE)
        def _(b):
            at = pl.multiple_of(b * TILE, TILE)
            w_buf[i % DEPTH, pl.ds(at, TILE), :] = gathered[pl.ds(i * PART + at, TILE), :].astype(
                jnp.float32
            )

        w_copy(i).start()

    def scan(src, kept):
        def one(k, carry):
            kept, here = carry
            g = src * local + k
            mine = (owners[g] == me).astype(jnp.int32)
            matrix_at[kept] = g
            slot_at[kept] = src * 2 + here
            return kept + mine, here + mine

        return lax.fori_loop(0, local, one, (kept, jnp.int32(0)))[0]

    def pick(j, count):
        @pl.when(j < count)
        def _():
            w_part = pl.ds(pl.multiple_of(matrix_at[j] * BLOCK, BLOCK), BLOCK)
            fresh = average_decay * unpacked[slot_at[j]].astype(jnp.float32) + (
                1.0 - average_decay
            ) * gathered[w_part, :].astype(jnp.float32)
            fresh_buf[j] = fresh.astype(jnp.bfloat16)

        @pl.when(j >= count)
        def _():
            fresh_buf[j] = jnp.zeros(fresh_buf.shape[1:], jnp.bfloat16)

        fresh_copy(j).start()

    for copy in state:
        copy.start()
    for i in range(DEPTH):
        widen(i)
    count = lax.fori_loop(0, n_dp, scan, jnp.int32(0))
    for j in range(most):
        pick(j, count)
    for i in range(DEPTH, parts):
        widen(i)
    for i in range(parts - DEPTH, parts):
        w_copy(i).wait()
    for j in range(most):
        fresh_copy(j).wait()
    for copy in state:
        copy.wait()


def grid_shards(n_dp, n_mp, limit, grads, weights, moment1, moment2, average, owners):
    shard, width = weights.shape
    local = shard // BLOCK
    most = local + local // 2
    nmat = owners.shape[0]
    total_rows = grads.shape[1]
    owner_col = pltpu.with_memory_space_constraint(owners[:, 0], pltpu.HBM)
    any_spec = pl.BlockSpec(memory_space=pl.ANY)
    smem_spec = pl.BlockSpec(memory_space=pltpu.SMEM)
    bf16, f32 = jnp.bfloat16, jnp.float32
    dma = pltpu.SemaphoreType.DMA

    average = average.reshape(local, BLOCK, width)
    grads, weights, moment1, moment2, average = (
        pltpu.with_memory_space_constraint(a, pltpu.HBM)
        for a in (grads, weights, moment1, moment2, average)
    )
    gathered, new_m, new_v, unpacked = pl.pallas_call(
        functools.partial(step_kernel, n_dp, n_mp, limit, nmat),
        out_shape=(
            pltpu.VMEM((total_rows, width), bf16),
            pltpu.VMEM((shard, width), f32),
            pltpu.VMEM((shard, width), f32),
            pltpu.VMEM((n_dp * 2, BLOCK, width), bf16),
        ),
        in_specs=[smem_spec] + [any_spec] * 5,
        out_specs=(any_spec,) * 4,
        scratch_shapes=[
            pltpu.VMEM((4, shard, width), bf16),
            pltpu.VMEM((4, shard, width), bf16),
            pltpu.VMEM((5, shard, width), bf16),
            pltpu.VMEM((shard, width), f32),
            pltpu.VMEM((shard, width), f32),
            pltpu.VMEM((shard, width), f32),
            pltpu.VMEM((shard, width), f32),
            pltpu.VMEM((shard, width), bf16),
            pltpu.VMEM((n_dp, 8, width // 2), f32),
            pltpu.VMEM((n_mp, 8, width // 2), f32),
            pltpu.VMEM((shard, width), bf16),
            pltpu.VMEM((shard, width), bf16),
            pltpu.VMEM((local, BLOCK, width), bf16),
            pltpu.VMEM((n_dp * 2, BLOCK, width), bf16),
            pltpu.VMEM((6, BLOCK, width), bf16),
            dma((9,)),
            dma,
            dma((4 * CHUNKS,)),
            dma,
            dma((5 * CHUNKS,)),
            dma,
            dma,
            dma,
            dma,
            dma,
            dma,
            dma,
            dma((3,)),
            dma,
            dma,
            dma,
            dma,
            dma((2,)),
            dma((2,)),
        ],
        compiler_params=pltpu.CompilerParams(
            collective_id=0, has_side_effects=True, vmem_limit_bytes=32 * 2**20
        ),
    )(owner_col, grads, weights, moment1, moment2, average)

    gathered, new_m, new_v, unpacked = (
        pltpu.with_memory_space_constraint(a, pltpu.VMEM) for a in (gathered, new_m, new_v, unpacked)
    )
    vmem_spec = pl.BlockSpec(memory_space=pltpu.VMEM)
    new_full, owned, new_m, new_v = pl.pallas_call(
        functools.partial(finish_kernel, n_dp, most, nmat),
        out_shape=(
            jax.ShapeDtypeStruct((total_rows, width), f32),
            jax.ShapeDtypeStruct((1, most * BLOCK, width), bf16),
            jax.ShapeDtypeStruct((shard, width), f32),
            jax.ShapeDtypeStruct((shard, width), f32),
        ),
        in_specs=[smem_spec, vmem_spec, vmem_spec, any_spec, any_spec],
        out_specs=(any_spec,) * 4,
        scratch_shapes=[
            pltpu.VMEM((DEPTH, PART, width), f32),
            pltpu.VMEM((most, BLOCK, width), bf16),
            pltpu.SMEM((most + 1,), jnp.int32),
            pltpu.SMEM((most + 1,), jnp.int32),
            dma((DEPTH,)),
            dma((most,)),
            dma((2,)),
        ],
        compiler_params=pltpu.CompilerParams(vmem_limit_bytes=16 * 2**20),
    )(owner_col, gathered, unpacked, new_m, new_v)
    return (new_full, new_m, new_v, owned)


def solution(mesh):
    n_dp, n_mp = mesh.shape["dp"], mesh.shape["mp"]

    def step(grads, weights, moment1, moment2, average, owners):
        limit = float(weights.shape[0] * weights.shape[1]) ** 0.5
        if n_dp == 8:
            body = functools.partial(grid_shards, n_dp, n_mp, limit)
        else:
            body = functools.partial(plain_shards, limit)
        placed = (P("dp", None, "mp"), P("dp", "mp"), P("dp", "mp"), P("dp", "mp"), P("dp", "mp"), P())
        return jax.shard_map(
            body,
            mesh=mesh,
            in_specs=placed,
            out_specs=(P(None, "mp"), P("dp", "mp"), P("dp", "mp"), P("dp", None, "mp")),
            check_vma=False,
        )(grads, weights, moment1, moment2, average, owners)

    return step
```
